512 devices in a mesh: grp: 8 (over y), ctx: 64 (over z, x, core).
Axes of the slice: x: 4, y: 8, z: 8, core: 2. Of those that a mesh axis runs over, the one named last changes fastest.
Arguments:
- tokens: bfloat16 [65536, 2048], P(('grp', 'ctx')), parts along dimension 0, may hold values from -32 to 32
- gain_in: float32 [2048], replicated, may hold values from 0.1 to 1.9
- long_filter: bfloat16 [2048, 8192], P('ctx'), may hold values from -0.0625 to 0.0625
- skip_gain: float32 [2048], P('ctx'), may hold values from 0.5 to 1.5
- gain_ffn: float32 [2048], replicated, may hold values from 0.1 to 1.9
- router: bfloat16 [2048, 16], replicated, may hold values from -1 to 1
- w_up: bfloat16 [2048, 16384], P(None, 'ctx'), may hold values from -0.125 to 0.125
- w_down: bfloat16 [16384, 2048], P('ctx'), may hold values from -0.375 to 0.375
- expert_id: int32 [65536], P(('grp', 'ctx')), parts along dimension 0, may hold values from 0 to 15
- slot_index: int32 [65536], P(('grp', 'ctx')), parts along dimension 0, may hold values from 0 to 15, as said below
Outputs:
- layer_out: bfloat16 [65536, 2048], P(('grp', 'ctx')), parts along dimension 0
The draws below stay inside these ranges and needn't reach their ends.
There are 8 independent parts, one for each index of `grp`. The reference program is written for one: setup_inputs(seed, part) draws one part's arguments, and reference() takes and returns one part's arrays. A program takes and returns all parts, laid end to end along the dimension named above; an argument that names none is the same for every part. Nothing has to cross between parts.
Inputs may be any that keep to these rules, and one draw needn't show every extreme that they name: Among the 128 tokens of one device no two share both expert_id and slot_index; one expert, the same for all devices, receives 4 * 4 tokens from every device; the others receive at most as many.
All inputs are finite; a program needn't handle non-finite values.
Results may differ from the reference program's by a relative error of at most 0.0085.
Values may be sent and summed in bfloat16 or wider, within the bound.
A program may use at most 64 MiB of HBM per device.

```python
import math
import jax
import jax.numpy as jnp
from jax import lax

D = 2048
FF = 1024
TOK_DEV = 128
QUAD = 4
EXPERTS = 16
CAP = 4
TOKENS = 8192
N_CTX = 64


def feature_sign():
    index = jnp.arange(D, dtype=jnp.int32)
    return (1 - 2 * (index * 40503 // 256 % 2)).astype(jnp.float32)


def draw_tokens(key, part):
    k_noise, k_column, k_row = jax.random.split(key, 3)
    noise = jnp.clip(jax.random.normal(k_noise, (TOKENS, D), jnp.float32), -5.0, 5.0)
    column_scale = 0.2 * jnp.exp(jax.random.uniform(k_column, (1, D), jnp.float32, 0.0, math.log(10.0)))
    row_scale = 0.3 * jnp.exp(jax.random.uniform(k_row, (TOKENS, 1), jnp.float32, 0.0, math.log(10.0)))
    shared = 0.33 * feature_sign()[None, :]
    return ((noise * column_scale + shared) * row_scale).astype(jnp.bfloat16)


def draw_router(key, part):
    noise = jnp.clip(jax.random.normal(jax.random.fold_in(key, 41), (D, EXPERTS), jnp.float32), -5.0, 5.0)
    aligned = 10.0 / D * feature_sign()[:, None]
    return (noise * (1.0 / math.sqrt(D)) + aligned).astype(jnp.bfloat16)


def route_flat(key):
    bucket = QUAD * CAP
    blocks = TOKENS // TOK_DEV
    busiest = jax.random.randint(jax.random.fold_in(key, 11), (), 0, EXPERTS).astype(jnp.int32)
    base_key = jax.random.fold_in(key, 23)

    def one_block(index):
        block_key = jax.random.fold_in(base_key, index)
        k_order, k_full, k_rest = jax.random.split(block_key, 3)
        order = jax.random.permutation(k_order, TOK_DEV).astype(jnp.int32)
        full_slots = jax.random.permutation(k_full, bucket).astype(jnp.int32)
        rest_slots = jax.random.permutation(k_rest, (EXPERTS - 1) * bucket).astype(jnp.int32)[:TOK_DEV - bucket]
        rest_expert = rest_slots // bucket
        rest_expert = rest_expert + (rest_expert >= busiest).astype(jnp.int32)
        targets = jnp.concatenate([busiest * bucket + full_slots, rest_expert * bucket + rest_slots % bucket])
        return jnp.zeros((TOK_DEV,), jnp.int32).at[order].set(targets)
    flat_all = jax.vmap(one_block)(jnp.arange(blocks, dtype=jnp.int32))
    return flat_all.reshape(TOKENS)


def draw_expert_id(key, part):
    return route_flat(key) // (QUAD * CAP)


def draw_slot_index(key, part):
    return route_flat(key) % (QUAD * CAP)


def level_of(own_key, shape, cuts, smallest, largest):
    loudness, own = 1.0, jax.random.fold_in(own_key, 6)
    for dim, blocks in cuts:
        heights = jnp.exp(jax.random.uniform(jax.random.fold_in(own, dim), (blocks,), jnp.float32, smallest / len(cuts), largest / len(cuts)))
        loudness = loudness * jnp.repeat(heights, shape[dim] // blocks).reshape([-1 if axis == dim else 1 for axis in range(len(shape))])
    return loudness


def normal_values(own_key, shape, scale, reach, cuts=(), held_as=jnp.bfloat16):
    drawn = jax.random.normal(own_key, shape, jnp.float32) * scale
    if len(cuts) > 0:
        drawn = level_of(own_key, shape, cuts, -0.22, 0.18) * drawn
    return jnp.clip(drawn, min=-reach, max=reach).astype(held_as)


def setup_inputs(seed: int = 0, part: int = 0) -> dict:
    key_list = jax.random.split(jax.random.key(seed), 11)
    own_keys = jax.random.split(jax.random.fold_in(key_list[10], part), 11)
    return {
        "tokens": draw_tokens(jax.random.fold_in(jax.random.fold_in(key_list[10], part), 71), part),
        "gain_in": jnp.clip(1.0 + 0.18 * jax.random.normal(key_list[1], (D,), jnp.float32), 0.1, 1.9),
        "long_filter": normal_values(key_list[2], (D, TOKENS), TOKENS ** -0.5, 0.0625, ((0, 64),)),
        "skip_gain": jnp.clip(0.5 + 1.0 * jax.random.uniform(key_list[3], (D,), jnp.float32) ** level_of(key_list[3], (D,), ((0, 64),), -0.2, 0.2), 0.5, 1.5),
        "gain_ffn": jnp.clip(1.0 + 0.18 * jax.random.normal(key_list[4], (D,), jnp.float32), 0.1, 1.9),
        "router": draw_router(jax.random.fold_in(key_list[10], 71), part),
        "w_up": normal_values(key_list[6], (D, EXPERTS * FF), D ** -0.5, 0.125, ((1, 64),)),
        "w_down": normal_values(key_list[7], (EXPERTS * FF, D), (FF // 4) ** -0.5, 0.375, ((0, 64),)),
        "expert_id": draw_expert_id(jax.random.fold_in(jax.random.fold_in(key_list[10], part), 71), part),
        "slot_index": draw_slot_index(jax.random.fold_in(jax.random.fold_in(key_list[10], part), 71), part),
    }


def rms_scale(values, gain):
    floats = values.astype(jnp.float32)
    return floats * lax.rsqrt(lax.optimization_barrier(jnp.mean(floats * floats, axis=1, keepdims=True)) + 1e-06) * gain

def reference(tokens, gain_in, long_filter, skip_gain, gain_ffn, router, w_up, w_down, expert_id, slot_index):
    normed = rms_scale(tokens, gain_in).astype(jnp.bfloat16)
    signal = normed.astype(jnp.float32)
    kernel = long_filter.astype(jnp.float32).T
    length_two = 2 * TOKENS
    spectrum = jnp.fft.rfft(signal, n=length_two, axis=0) * jnp.fft.rfft(kernel, n=length_two, axis=0)
    convolved = jnp.fft.irfft(spectrum, n=length_two, axis=0)[:TOKENS]
    conv_out = (convolved + skip_gain * signal).astype(jnp.bfloat16)
    middle = (tokens.astype(jnp.float32) + conv_out.astype(jnp.float32)).astype(jnp.bfloat16)
    ffn_in = rms_scale(middle, gain_ffn).astype(jnp.bfloat16)
    logits = jnp.dot(ffn_in, router, preferred_element_type=jnp.float32)
    gate_value = jax.nn.sigmoid(jnp.take_along_axis(logits, expert_id[:, None], axis=1)[:, 0])
    source = (jnp.arange(TOKENS, dtype=jnp.int32) // TOK_DEV).astype(jnp.int32)
    buckets = jnp.zeros((EXPERTS, N_CTX, QUAD * CAP, D), jnp.bfloat16)
    buckets = buckets.at[expert_id, source, slot_index].set(ffn_in)
    up_each = w_up.reshape(D, EXPERTS, FF).transpose(1, 0, 2)
    down_each = w_down.reshape(EXPERTS, FF, D)

    def one_expert(operands):
        bucket_rows, up_one, down_one = operands
        flat_rows = bucket_rows.reshape(N_CTX * QUAD * CAP, D)
        hidden = jax.nn.gelu(jnp.dot(flat_rows, up_one, preferred_element_type=jnp.float32), approximate=False).astype(jnp.bfloat16)
        result = jnp.dot(hidden, down_one, preferred_element_type=jnp.float32).astype(jnp.bfloat16)
        return result.reshape(N_CTX, QUAD * CAP, D)
    results = lax.map(one_expert, (buckets, up_each, down_each))
    expert_out = results[expert_id, source, slot_index].astype(jnp.float32)
    layer_out = (middle.astype(jnp.float32) + gate_value[:, None] * expert_out).astype(jnp.bfloat16)
    return layer_out
```

```python
import functools
import math

import jax
import jax.numpy as jnp
from jax import lax
from jax.experimental import pallas as pl
from jax.experimental.pallas import tpu as pltpu
from jax.sharding import PartitionSpec as P

MESH = pl.DeviceIdType.MESH


def angle_table(first, second, period):
    product = first[:, None] * second[None, :] % period
    angles = product.astype(jnp.float32) * (2.0 * math.pi / period)
    return (jnp.cos(angles), jnp.sin(angles))


def enter(peers, me, n):
    barrier = pltpu.get_barrier_semaphore()

    def greet(i, carry):
        pl.semaphore_signal(
            barrier, inc=1, device_id={"ctx": lax.rem(me + i, n)}, device_id_type=MESH
        )
        return carry

    lax.fori_loop(1, n, greet, 0)
    pl.semaphore_wait(barrier, n - 1)


def class_of(dev):
    z, x, core = dev // 8, dev // 2 % 4, dev % 2
    parity = (x + x // 2) % 2
    return parity * 2 + core, z * 2 + x // 2


def owner_class(dev):
    x, core = dev // 2 % 4, dev % 2
    return (x + x // 2) % 2 * 2 + core


def source_of(dev, rank):
    x, core = dev // 2 % 4, dev % 2
    parity = (x + x // 2) % 2
    src_x = parity + rank % 2 * (3 - 2 * parity)
    return (rank // 2 * 4 + src_x) * 2 + core


def spread_kernel(n, toks, aux, toks_out, aux_out, local, s_tok, r_tok, s_aux, r_aux):
    me = lax.axis_index("ctx")
    enter(None, me, n)
    group, rank = class_of(me)
    place = group * 16 + rank

    def tok_copy(peer, slot):
        return pltpu.make_async_remote_copy(
            toks.at[peer], toks_out.at[place], s_tok.at[peer], r_tok.at[slot],
            device_id={"ctx": peer}, device_id_type=MESH)

    def aux_copy(peer, slot):
        return pltpu.make_async_remote_copy(
            aux, aux_out.at[place], s_aux.at[peer], r_aux.at[slot],
            device_id={"ctx": peer}, device_id_type=MESH)

    def send(i, carry):
        peer = lax.rem(me + i, n)
        aux_copy(peer, me).start()
        tok_copy(peer, me).start()
        return carry

    lax.fori_loop(1, n, send, 0)
    own = [
        pltpu.make_async_copy(toks.at[me], toks_out.at[place], local.at[0]),
        pltpu.make_async_copy(aux, aux_out.at[place], local.at[1]),
    ]
    for copy in own:
        copy.start()
    for copy in own:
        copy.wait()

    def finish(i, carry):
        peer = lax.rem(me + i, n)
        aux_copy(peer, peer).wait()
        tok_copy(peer, peer).wait()
        return carry

    lax.fori_loop(1, n, finish, 0)


def spread(toks, aux, n):
    return pl.pallas_call(
        functools.partial(spread_kernel, n),
        out_shape=(
            jax.ShapeDtypeStruct(toks.shape, toks.dtype),
            jax.ShapeDtypeStruct((n,) + aux.shape, aux.dtype),
        ),
        in_specs=[pl.BlockSpec(memory_space=pl.ANY)] * 2,
        out_specs=[pl.BlockSpec(memory_space=pl.ANY)] * 2,
        scratch_shapes=[
            pltpu.SemaphoreType.DMA((2,)),
            pltpu.SemaphoreType.DMA((n,)),
            pltpu.SemaphoreType.DMA((n,)),
            pltpu.SemaphoreType.DMA((n,)),
            pltpu.SemaphoreType.DMA((n,)),
        ],
        compiler_params=pltpu.CompilerParams(collective_id=0, has_side_effects=True),
    )(toks, aux)


def dispatch_kernel(n, rows, rows_out, local, s_sem, r_sem):
    me = lax.axis_index("ctx")
    enter(None, me, n)

    def row_copy(peer, slot):
        return pltpu.make_async_remote_copy(
            rows.at[owner_class(peer), peer // 4], rows_out.at[me], s_sem.at[peer], r_sem.at[slot],
            device_id={"ctx": peer}, device_id_type=MESH)

    def send(i, carry):
        row_copy(lax.rem(me + i, n), me).start()
        return carry

    lax.fori_loop(1, n, send, 0)
    own = pltpu.make_async_copy(rows.at[owner_class(me), me // 4], rows_out.at[me], local)
    own.start()
    own.wait()

    def finish(i, carry):
        peer = lax.rem(me + i, n)
        row_copy(peer, peer).wait()
        return carry

    lax.fori_loop(1, n, finish, 0)


def dispatch(rows, n):
    return pl.pallas_call(
        functools.partial(dispatch_kernel, n),
        out_shape=jax.ShapeDtypeStruct((n,) + rows.shape[2:], rows.dtype),
        in_specs=[pl.BlockSpec(memory_space=pl.ANY)],
        out_specs=pl.BlockSpec(memory_space=pl.ANY),
        scratch_shapes=[
            pltpu.SemaphoreType.DMA,
            pltpu.SemaphoreType.DMA((n,)),
            pltpu.SemaphoreType.DMA((n,)),
        ],
        compiler_params=pltpu.CompilerParams(collective_id=1, has_side_effects=True),
    )(rows)


def combine_kernel(n, rows, rows_out, local, s_sem, r_sem):
    me = lax.axis_index("ctx")
    enter(None, me, n)
    expert = me // 4
    group, my_rank = class_of(me)
    core, parity = me % 2, group // 2

    def holder(other):
        pair = other % 2
        return (other // 2 * 4 + 2 * pair + (parity + pair) % 2) * 2 + core

    def row_copy(rank, slot):
        return pltpu.make_async_remote_copy(
            rows.at[rank], rows_out.at[expert], s_sem.at[rank], r_sem.at[slot],
            device_id={"ctx": source_of(me, rank)}, device_id_type=MESH)

    def send(rank, carry):
        @pl.when(source_of(me, rank) != me)
        def _():
            row_copy(rank, expert).start()
        return carry

    lax.fori_loop(0, 16, send, 0)

    @pl.when(source_of(me, my_rank) == me)
    def _():
        own = pltpu.make_async_copy(rows.at[my_rank], rows_out.at[expert], local)
        own.start()
        own.wait()

    def finish(i, carry):
        @pl.when(source_of(me, i) != me)
        def _():
            row_copy(i, i).wait_send()

        @pl.when(holder(i) != me)
        def _():
            row_copy(0, i).wait_recv()
        return carry

    lax.fori_loop(0, 16, finish, 0)


def combine(rows, n):
    return pl.pallas_call(
        functools.partial(combine_kernel, n),
        out_shape=jax.ShapeDtypeStruct(rows.shape, rows.dtype),
        in_specs=[pl.BlockSpec(memory_space=pl.ANY)],
        out_specs=pl.BlockSpec(memory_space=pl.ANY),
        scratch_shapes=[
            pltpu.SemaphoreType.DMA,
            pltpu.SemaphoreType.DMA((16,)),
            pltpu.SemaphoreType.DMA((16,)),
        ],
        compiler_params=pltpu.CompilerParams(collective_id=2, has_side_effects=True),
    )(rows)


def tables(order):
    quarter = 4 * jnp.arange(64, dtype=jnp.int32) + 1
    lane = jnp.arange(128, dtype=jnp.int32)
    cos_outer, sin_outer = angle_table(order, quarter, 256)
    cos_twist, sin_twist = angle_table(quarter, lane, 32768)
    cos_inner, sin_inner = angle_table(lane, lane, 128)
    return cos_outer, sin_outer, cos_twist, sin_twist, cos_inner, sin_inner


def dot_high(left, right):
    return jnp.dot(left, right, precision=lax.Precision.HIGH, preferred_element_type=jnp.float32)


def forward(blocks, spec, order):
    cos_outer, sin_outer, cos_twist, sin_twist, cos_inner, sin_inner = tables(order)
    outer = jnp.concatenate([cos_outer, -sin_outer], axis=1)
    first = jnp.einsum(spec, blocks, outer, precision=lax.Precision.HIGH)
    re, im = first[:, :64], first[:, 64:]
    twisted = jnp.concatenate(
        [re * cos_twist + im * sin_twist, im * cos_twist - re * sin_twist], axis=2)
    inner = jnp.concatenate(
        [
            jnp.concatenate([cos_inner, -sin_inner], axis=1),
            jnp.concatenate([sin_inner, cos_inner], axis=1),
        ],
        axis=0,
    )
    return dot_high(twisted.reshape(-1, 256), inner).reshape(-1, 64, 256)


def inverse(prod, order):
    cos_outer, sin_outer, cos_twist, sin_twist, cos_inner, sin_inner = tables(order)
    inner = jnp.concatenate(
        [
            jnp.concatenate([cos_inner, sin_inner], axis=1),
            jnp.concatenate([-sin_inner, cos_inner], axis=1),
        ],
        axis=0,
    )
    back = dot_high(prod.reshape(-1, 256), inner).reshape(-1, 64, 256)
    re, im = back[:, :, :128], back[:, :, 128:]
    turned = jnp.concatenate(
        [re * cos_twist - im * sin_twist, im * cos_twist + re * sin_twist], axis=1)
    outer = jnp.concatenate([cos_outer, -sin_outer], axis=1) / 8192.0
    return jnp.einsum("ckn,pk->cpn", turned, outer, precision=lax.Precision.HIGH)


def swapped(array, bit):
    return lax.ppermute(array, "ctx", [(i, i ^ (1 << bit)) for i in range(64)])


def body(
    tokens, gain_in, long_filter, skip_gain, gain_ffn, router, w_up, w_down, expert_id, slot_index
):
    n = lax.axis_size("ctx")
    me = lax.axis_index("ctx")
    far_up, far_down = swapped(w_up, 1), swapped(w_down, 1)
    ups = [w_up, swapped(w_up, 0), far_up, swapped(far_up, 0)]
    downs = [w_down, swapped(w_down, 0), far_down, swapped(far_down, 0)]

    floats = tokens.astype(jnp.float32)
    scale = lax.rsqrt(jnp.mean(floats * floats, axis=1) + 1e-06)
    target = expert_id * 16 + slot_index
    aux = jnp.stack([scale, target.astype(jnp.float32)], axis=0)
    toks, auxes = spread(tokens.T.reshape(n, 32, 128), aux, n)

    place = jnp.arange(64, dtype=jnp.int32)
    parity, core, rank = place // 32, place // 16 % 2, place % 16
    order = (rank // 2 * 4 + parity + rank % 2 * (3 - 2 * parity)) * 2 + core

    gain = lax.dynamic_slice(gain_in, (me * 32,), (32,))
    tok_f = toks.astype(jnp.float32)
    normed = (tok_f * auxes[:, 0][:, None, :] * gain[None, :, None]).astype(jnp.bfloat16)
    normed = normed.astype(jnp.float32)
    spec_f = forward(
        long_filter.astype(jnp.float32).reshape(32, 64, 128), "cpn,pk->ckn",
        jnp.arange(64, dtype=jnp.int32))
    spec_x = forward(normed, "pcn,pk->ckn", order)
    x_re, x_im = spec_x[:, :, :128], spec_x[:, :, 128:]
    f_re, f_im = spec_f[:, :, :128], spec_f[:, :, 128:]
    prod = jnp.concatenate([x_re * f_re - x_im * f_im, x_re * f_im + x_im * f_re], axis=2)
    conv = inverse(prod, order)
    conv_out = (conv.transpose(1, 0, 2) + skip_gain[None, :, None] * normed).astype(jnp.bfloat16)
    middle = (tok_f + conv_out.astype(jnp.float32)).astype(jnp.bfloat16)

    chosen = auxes[:, 1].astype(jnp.int32)
    onehot = (
        lax.broadcasted_iota(jnp.int32, (64, 256, 128), 1) == chosen[:, None, :]
    ).astype(jnp.bfloat16)
    packed = jnp.einsum("pst,pct->psc", onehot, middle, preferred_element_type=jnp.float32)
    packed = packed.astype(jnp.bfloat16).reshape(4, 4, 4, 16, 16, 32)
    packed = packed.transpose(0, 3, 1, 4, 2, 5).reshape(4, 16, 64, 128)
    received = dispatch(packed, n)
    mid_rows = received.reshape(64, 4, 16, 4, 32).transpose(1, 3, 2, 0, 4).reshape(256, 2048)

    rows_f = mid_rows.astype(jnp.float32)
    row_scale = lax.rsqrt(jnp.mean(rows_f * rows_f, axis=1, keepdims=True) + 1e-06)
    ffn_in = (rows_f * row_scale * gain_ffn).astype(jnp.bfloat16)
    logits = jnp.dot(ffn_in, router, preferred_element_type=jnp.float32)
    mine = lax.broadcasted_iota(jnp.int32, logits.shape, 1) == me // 4
    gate_value = jax.nn.sigmoid(jnp.sum(jnp.where(mine, logits, 0.0), axis=1, keepdims=True))
    total = jnp.zeros((256, 2048), jnp.float32)
    for up, down in zip(ups, downs):
        hidden = jax.nn.gelu(
            jnp.dot(ffn_in, up, preferred_element_type=jnp.float32), approximate=False
        ).astype(jnp.bfloat16)
        total = total + jnp.dot(hidden, down, preferred_element_type=jnp.float32)
    expert_out = total.astype(jnp.bfloat16).astype(jnp.float32)
    out_rows = (rows_f + gate_value * expert_out).astype(jnp.bfloat16)
    arrived = combine(out_rows.reshape(16, 16, 2048), n)
    pick = (
        lax.broadcasted_iota(jnp.int32, (128, 256), 1) == target[:, None]
    ).astype(jnp.bfloat16)
    return jnp.dot(
        pick, arrived.reshape(256, 2048), preferred_element_type=jnp.float32
    ).astype(jnp.bfloat16)


def solution(mesh):
    return jax.shard_map(
        body,
        mesh=mesh,
        in_specs=(
            P(("grp", "ctx"), None),
            P(),
            P("ctx", None),
            P("ctx"),
            P(),
            P(),
            P(None, "ctx"),
            P("ctx", None),
            P(("grp", "ctx")),
            P(("grp", "ctx")),
        ),
        out_specs=P(("grp", "ctx"), None),
        check_vma=False,
    )
```

```python
import functools
import math

import jax
import jax.numpy as jnp
import numpy as np
from jax import lax
from jax.experimental import pallas as pl
from jax.experimental.pallas import tpu as pltpu
from jax.sharding import PartitionSpec as P

MESH = pl.DeviceIdType.MESH
F32, BF16 = jnp.float32, jnp.bfloat16
N = 64
GRP = 8


def class_of(dev):
    z, x, core = dev // 8, dev // 2 % 4, dev % 2
    return (x + x // 2) % 2 * 2 + core, z * 2 + x // 2


def owner_class(dev):
    x, core = dev // 2 % 4, dev % 2
    return (x + x // 2) % 2 * 2 + core


def source_of(dev, rank):
    x, core = dev // 2 % 4, dev % 2
    parity = (x + x // 2) % 2
    return (rank // 2 * 4 + parity + rank % 2 * (3 - 2 * parity)) * 2 + core


def holder_of(dev, expert):
    x, core = dev // 2 % 4, dev % 2
    pair = expert % 2
    return (expert // 2 * 4 + 2 * pair + (x + x // 2 + pair) % 2) * 2 + core


def split(table):
    high = table.astype(np.float32).astype(BF16)
    low = (table - high.astype(np.float64)).astype(np.float32).astype(BF16)
    return high, low


@functools.lru_cache(None)
def tables():
    place = np.arange(N)
    parity, core, rank = place // 32, place // 16 % 2, place % 16
    order = (rank // 2 * 4 + parity + rank % 2 * (3 - 2 * parity)) * 2 + core
    quarter = 4 * np.arange(64) + 1
    lane = np.arange(128)

    def angle(first, second, period):
        return 2.0 * math.pi * (np.outer(first, second) % period) / period

    twist = angle(quarter, lane, 32768)
    inner = angle(lane, lane, 128)
    ci, si = np.cos(inner), np.sin(inner)
    out = {"twist": np.stack([np.cos(twist), np.sin(twist)]).astype(np.float32)}
    for name, blocks in (("filt", np.arange(64)), ("sig", order)):
        theta = angle(quarter, blocks, 256)
        high, low = split(np.concatenate([np.cos(theta), -np.sin(theta)], axis=0))
        out["outer_" + name] = np.concatenate([high, low], axis=1)
    theta = angle(order, quarter, 256)
    high, low = split(np.concatenate([np.cos(theta), -np.sin(theta)], axis=1) / 8192.0)
    out["outer_inv"] = np.concatenate([high, low, high], axis=1)
    out["inner"] = np.stack(
        split(np.block([[ci, -si], [si, ci]])) + split(np.block([[ci, si], [-si, ci]])))
    return out


def dot(left, right):
    return jnp.dot(left, right, preferred_element_type=F32)


def halves(value):
    high = value.astype(BF16)
    return high, (value - high.astype(F32)).astype(BF16)


def kernel(
    tokens, target, chan, filt, gain_ffn, router, w_up, w_down,
    twist, outer_filt, outer_sig, outer_inv, inner,
    out,
    toks_t, aux, toks, auxes, stage, spec, high, low, diag, packed, rows, mid, ffn_in, hidden,
    out_rows, arrived, up, down,
    s_tok, r_tok, s_aux, r_aux, s_row, r_row, s_out, r_out, s_w, r_w, local,
):
    me = lax.axis_index("ctx")
    grp = lax.axis_index("grp")
    group, my_rank = class_of(me)
    place = group * 16 + my_rank
    expert = me // 4
    partner = me // 2 * 2 + 1 - me % 2
    across = me // 4 * 4 + (me + 2) % 4
    ahead, behind = lax.rem(grp + 1, GRP), lax.rem(grp + GRP - 1, GRP)

    barrier = pltpu.get_barrier_semaphore()

    def greet(i, carry):
        pl.semaphore_signal(
            barrier, inc=1, device_id={"ctx": lax.rem(me + i, N)}, device_id_type=MESH)
        return carry

    lax.fori_loop(1, N, greet, 0)
    for neighbour in (ahead, behind):
        pl.semaphore_signal(barrier, inc=1, device_id={"grp": neighbour}, device_id_type=MESH)

    own_up = pltpu.make_async_copy(w_up, up.at[0], local.at[0])
    own_down = pltpu.make_async_copy(w_down, down.at[pl.ds(0, 256)], local.at[1])
    own_up.start()
    own_down.start()

    total = jnp.zeros((1, 128), F32)
    for j in range(16):
        block = tokens[:, 128 * j : 128 * j + 128].astype(F32).T
        total = total + jnp.sum(block * block, axis=0, keepdims=True)
        toks_t[4 * j : 4 * j + 4] = block.astype(BF16).reshape(4, 32, 128)
    aux[0:1, :] = lax.rsqrt(total * (1.0 / 2048.0) + 1e-06)
    aux[1:2, :] = target[...]
    pl.semaphore_wait(barrier, N + 1)

    def tok_copy(peer, slot):
        return pltpu.make_async_remote_copy(
            toks_t.at[peer], toks.at[place], s_tok.at[peer], r_tok.at[slot],
            device_id={"ctx": peer}, device_id_type=MESH)

    def aux_copy(peer, slot):
        return pltpu.make_async_remote_copy(
            aux, auxes.at[place], s_aux.at[peer], r_aux.at[slot],
            device_id={"ctx": peer}, device_id_type=MESH)

    def send_toks(i, carry):
        peer = lax.rem(me + i, N)
        aux_copy(peer, me).start()
        tok_copy(peer, me).start()
        return carry

    lax.fori_loop(1, N, send_toks, 0)

    def eighth(source_up, source_down, idx, device, sems):
        ups = pl.ds(idx * 256, 256)
        return [
            pltpu.make_async_remote_copy(
                source_up.at[ups], up.at[2, ups], s_w.at[sems], r_w.at[sems],
                device_id=device, device_id_type=MESH),
            pltpu.make_async_remote_copy(
                source_down(idx), down.at[pl.ds(512 + idx * 32, 32)], s_w.at[sems + 1],
                r_w.at[sems + 1], device_id=device, device_id_type=MESH),
        ]

    def start(copies):
        for copy in copies:
            copy.start()

    def wait(copies):
        for copy in copies:
            copy.wait()

    over_x = eighth(w_up, lambda i: w_down.at[pl.ds(i * 32, 32)], grp, {"ctx": across}, 0)
    start(over_x)
    on_chip = [
        pltpu.make_async_remote_copy(
            w_up, up.at[1], s_w.at[2], r_w.at[2], device_id={"ctx": partner},
            device_id_type=MESH),
        pltpu.make_async_remote_copy(
            w_down, down.at[pl.ds(256, 256)], s_w.at[3], r_w.at[3],
            device_id={"ctx": partner}, device_id_type=MESH),
    ]
    start(on_chip)

    def held(i):
        return down.at[pl.ds(512 + i * 32, 32)]

    def ring(step):
        forth = eighth(up.at[2], held, lax.rem(grp + GRP - step, GRP), {"grp": ahead}, 4 + 4 * step)
        if step == 3:
            return forth
        return forth + eighth(
            up.at[2], held, lax.rem(grp + step, GRP), {"grp": behind}, 6 + 4 * step)

    def transform(outer):
        def channels(i, carry):
            for j in range(4):
                at = pl.multiple_of((4 * i + j) * 64, 64)
                block = stage[pl.ds(at, 64), :].astype(BF16)
                first = dot(outer[...], jnp.concatenate([block, block], axis=0))
                re, im = first[:64], first[64:]
                ct, st = twist[0], twist[1]
                re_h, re_l = halves(re * ct + im * st)
                im_h, im_l = halves(im * ct - re * st)
                high[pl.ds(at, 64), 0:128] = re_h
                high[pl.ds(at, 64), 128:256] = im_h
                low[pl.ds(at, 64), 0:128] = re_l
                low[pl.ds(at, 64), 128:256] = im_l
            return carry

        lax.fori_loop(0, 8, channels, 0)

    def inner_dot(hi, lo, which):
        return dot(hi, inner[which]) + dot(hi, inner[which + 1]) + dot(lo, inner[which])

    def load_filter(i, carry):
        stage[pl.ds(i, 32, stride=64), :] = filt[
            :, pl.ds(pl.multiple_of(i * 128, 128), 128)].astype(F32)
        return carry

    lax.fori_loop(0, N, load_filter, 0)
    transform(outer_filt)

    def filter_inner(i, carry):
        at = pl.ds(pl.multiple_of(i * 512, 512), 512)
        spec[at, :] = inner_dot(high[at, :], low[at, :], 0)
        return carry

    lax.fori_loop(0, 4, filter_inner, 0)
    wait(over_x)
    start(ring(0))

    toks[pl.ds(place, 1)] = toks_t[pl.ds(me, 1)]
    auxes[pl.ds(place, 1)] = aux[...].reshape(1, 2, 128)

    def arrive(i, carry):
        peer = lax.rem(me + N - i, N)
        aux_copy(peer, peer).wait_recv()
        tok_copy(peer, peer).wait_recv()
        return carry

    lax.fori_loop(1, N, arrive, 0)

    def normed_of(i):
        tok = toks[i].astype(F32)
        return tok, (tok * auxes[i, 0:1, :] * chan[0]).astype(BF16).astype(F32)

    def load_signal(i, carry):
        stage[pl.ds(i, 32, stride=64), :] = normed_of(i)[1]
        return carry

    lax.fori_loop(0, N, load_signal, 0)
    wait(ring(0))
    start(ring(1))
    transform(outer_sig)

    def convolve(i, carry):
        at = pl.ds(pl.multiple_of(i * 512, 512), 512)
        sig = inner_dot(high[at, :], low[at, :], 0)
        fil = spec[at, :]
        s_re, s_im = sig[:, :128], sig[:, 128:]
        f_re, f_im = fil[:, :128], fil[:, 128:]
        prod = jnp.concatenate([s_re * f_re - s_im * f_im, s_re * f_im + s_im * f_re], axis=1)
        p_h, p_l = halves(prod)
        back = inner_dot(p_h, p_l, 2)
        for j in range(8):
            re, im = back[64 * j : 64 * j + 64, :128], back[64 * j : 64 * j + 64, 128:]
            ct, st = twist[0], twist[1]
            t_h, t_l = halves(jnp.concatenate([re * ct - im * st, im * ct + re * st], axis=0))
            stage[pl.ds(pl.multiple_of(i * 512 + 64 * j, 64), 64), :] = dot(
                outer_inv[...], jnp.concatenate([t_h, t_h, t_l], axis=0))
        return carry

    lax.fori_loop(0, 4, convolve, 0)
    wait(ring(1))
    start(ring(2))

    diag[...] = jnp.zeros_like(diag)
    slot_ids = lax.broadcasted_iota(jnp.int32, (256, 128), 0).astype(F32)

    def pack(i, carry):
        picks = []
        for j in range(4):
            idx = 4 * i + j
            tok, normed = normed_of(idx)
            conv = stage[pl.ds(idx, 32, stride=64), :]
            conv_out = (conv + chan[1] * normed).astype(BF16).astype(F32)
            diag[32 * j : 32 * j + 32, 128 * j : 128 * j + 128] = (tok + conv_out).astype(BF16)
            picks.append(jnp.where(slot_ids == auxes[idx, 1:2, :], 1.0, 0.0).astype(BF16))
        picked = lax.dot_general(
            jnp.concatenate(picks, axis=1), diag[...], (((1,), (1,)), ((), ())),
            preferred_element_type=F32)
        packed[i // 4, :, pl.ds(pl.multiple_of(i % 4 * 16, 16), 16), :] = (
            picked.astype(BF16).reshape(16, 16, 128))
        return carry

    lax.fori_loop(0, 16, pack, 0)

    def row_copy(peer, slot):
        return pltpu.make_async_remote_copy(
            packed.at[owner_class(peer), peer // 4], rows.at[me], s_row.at[peer], r_row.at[slot],
            device_id={"ctx": peer}, device_id_type=MESH)

    def send_rows(i, carry):
        row_copy(lax.rem(me + i, N), me).start()
        return carry

    lax.fori_loop(1, N, send_rows, 0)
    wait(ring(2))
    start(ring(3))
    rows[pl.ds(me, 1)] = packed[group, pl.ds(expert, 1)]
    wait(ring(3))
    relay = [
        pltpu.make_async_remote_copy(
            up.at[2], up.at[3], s_w.at[18], r_w.at[18], device_id={"ctx": partner},
            device_id_type=MESH),
        pltpu.make_async_remote_copy(
            down.at[pl.ds(512, 256)], down.at[pl.ds(768, 256)], s_w.at[19], r_w.at[19],
            device_id={"ctx": partner}, device_id_type=MESH),
    ]
    start(relay)

    def rows_arrive(i, carry):
        peer = lax.rem(me + N - i, N)
        row_copy(peer, peer).wait_recv()
        return carry

    lax.fori_loop(1, N, rows_arrive, 0)

    lane = lax.broadcasted_iota(jnp.int32, (16, 128), 1)
    in_half, in_quarter = lane < 64, lane % 64 < 32

    def unpack(i, carry):
        at = pl.ds(pl.multiple_of(i * 128, 128), 128)
        for r in range(4):
            v = [rows[4 * i + j, 16 * r : 16 * r + 16, :].astype(F32) for j in range(4)]
            a0 = jnp.where(in_half, v[0], pltpu.roll(v[2], 64, 1))
            a1 = jnp.where(in_half, v[1], pltpu.roll(v[3], 64, 1))
            a2 = jnp.where(in_half, pltpu.roll(v[0], 64, 1), v[2])
            a3 = jnp.where(in_half, pltpu.roll(v[1], 64, 1), v[3])
            u = [
                jnp.where(in_quarter, a0, pltpu.roll(a1, 32, 1)),
                jnp.where(in_quarter, pltpu.roll(a0, 96, 1), a1),
                jnp.where(in_quarter, a2, pltpu.roll(a3, 32, 1)),
                jnp.where(in_quarter, pltpu.roll(a2, 96, 1), a3),
            ]
            for p in range(4):
                mid[64 * r + 16 * p : 64 * r + 16 * p + 16, at] = u[p]
        return carry

    lax.fori_loop(0, 16, unpack, 0)

    def norm_rows(i, carry):
        at = pl.ds(pl.multiple_of(i * 32, 32), 32)
        block = mid[at, :]
        scale = lax.rsqrt(
            jnp.sum(block * block, axis=1, keepdims=True) * (1.0 / 2048.0) + 1e-06)
        ffn_in[at, :] = (block * scale * gain_ffn[...]).astype(BF16)
        return carry

    lax.fori_loop(0, 8, norm_rows, 0)
    logits = dot(ffn_in[...], router[...])
    chosen = lax.broadcasted_iota(jnp.int32, logits.shape, 1) == expert
    gate = jax.nn.sigmoid(jnp.sum(jnp.where(chosen, logits, 0.0), axis=1, keepdims=True))

    own_up.wait()
    own_down.wait()
    wait(on_chip)
    wait(relay)

    def go_up(i, carry):
        value = dot(ffn_in[...], up[i])
        value = value * (1.0 + lax.erf(value * math.sqrt(0.5))) * 0.5
        hidden[:, pl.ds(pl.multiple_of(i * 256, 256), 256)] = value.astype(BF16)
        return carry

    lax.fori_loop(0, 4, go_up, 0)

    def go_down(i, carry):
        at = pl.ds(pl.multiple_of(i * 256, 256), 256)
        result = dot(hidden[...], down[:, at]).astype(BF16).astype(F32)
        out_rows[:, :, at] = (mid[:, at] + gate * result).astype(BF16).reshape(16, 16, 256)
        return carry

    lax.fori_loop(0, 8, go_down, 0)

    def out_copy(rank, slot):
        return pltpu.make_async_remote_copy(
            out_rows.at[rank], arrived.at[expert], s_out.at[rank], r_out.at[slot],
            device_id={"ctx": source_of(me, rank)}, device_id_type=MESH)

    def send_out(rank, carry):
        @pl.when(source_of(me, rank) != me)
        def _():
            out_copy(rank, expert).start()
        return carry

    lax.fori_loop(0, 16, send_out, 0)

    @pl.when(source_of(me, my_rank) == me)
    def _():
        arrived[pl.ds(expert, 1)] = out_rows[pl.ds(my_rank, 1)]

    pick = jnp.where(slot_ids == target[...], 1.0, 0.0).T.astype(BF16)

    def out_arrive(i, carry):
        @pl.when(holder_of(me, i) != me)
        def _():
            out_copy(0, i).wait_recv()
        return carry

    lax.fori_loop(0, 16, out_arrive, 0)

    def select(i, carry):
        at = pl.ds(pl.multiple_of(i * 256, 256), 256)
        out[:, at] = dot(pick, arrived[:, :, at].reshape(256, 256)).astype(BF16)
        return carry

    lax.fori_loop(0, 8, select, 0)

    def sent(i, carry):
        peer = lax.rem(me + i, N)
        aux_copy(peer, peer).wait_send()
        tok_copy(peer, peer).wait_send()
        row_copy(peer, peer).wait_send()
        return carry

    lax.fori_loop(1, N, sent, 0)

    def sent_out(rank, carry):
        @pl.when(source_of(me, rank) != me)
        def _():
            out_copy(rank, rank).wait_send()
        return carry

    lax.fori_loop(0, 16, sent_out, 0)


def body(
    tokens, gain_in, long_filter, skip_gain, gain_ffn, router, w_up, w_down, expert_id, slot_index
):
    me = lax.axis_index("ctx")
    target = (expert_id * 16 + slot_index).astype(F32).reshape(1, 128)
    gain = lax.dynamic_slice(gain_in, (me * 32,), (32,))
    chan = jnp.broadcast_to(jnp.stack([gain, skip_gain])[:, :, None], (2, 32, 128))
    t = tables()
    consts = [jnp.asarray(t[k]) for k in ("twist", "outer_filt", "outer_sig", "outer_inv", "inner")]
    vmem = pl.BlockSpec(memory_space=pltpu.VMEM)
    anywhere = pl.BlockSpec(memory_space=pl.ANY)
    dma = pltpu.SemaphoreType.DMA
    return pl.pallas_call(
        kernel,
        out_shape=jax.ShapeDtypeStruct((128, 2048), BF16),
        in_specs=[vmem] * 6 + [anywhere] * 2 + [vmem] * 5,
        out_specs=vmem,
        scratch_shapes=[
            pltpu.VMEM((N, 32, 128), BF16),
            pltpu.VMEM((2, 128), F32),
            pltpu.VMEM((N, 32, 128), BF16),
            pltpu.VMEM((N, 2, 128), F32),
            pltpu.VMEM((2048, 128), F32),
            pltpu.VMEM((2048, 256), F32),
            pltpu.VMEM((2048, 256), BF16),
            pltpu.VMEM((2048, 256), BF16),
            pltpu.VMEM((128, 512), BF16),
            pltpu.VMEM((4, 16, 64, 128), BF16),
            pltpu.VMEM((N, 64, 128), BF16),
            pltpu.VMEM((256, 2048), F32),
            pltpu.VMEM((256, 2048), BF16),
            pltpu.VMEM((256, 1024), BF16),
            pltpu.VMEM((16, 16, 2048), BF16),
            pltpu.VMEM((16, 16, 2048), BF16),
            pltpu.VMEM((4, 2048, 256), BF16),
            pltpu.VMEM((1024, 2048), BF16),
            dma((N,)), dma((N,)), dma((N,)), dma((N,)), dma((N,)), dma((N,)),
            dma((16,)), dma((16,)), dma((20,)), dma((20,)), dma((2,)),
        ],
        compiler_params=pltpu.CompilerParams(
            collective_id=0, has_side_effects=True, vmem_limit_bytes=60 * 1024 * 1024),
    )(
        tokens, target, chan, long_filter, gain_ffn.reshape(1, 2048), router, w_up, w_down, *consts
    )


def solution(mesh):
    return jax.shard_map(
        body,
        mesh=mesh,
        in_specs=(
            P(("grp", "ctx"), None),
            P(),
            P("ctx", None),
            P("ctx"),
            P(),
            P(),
            P(None, "ctx"),
            P("ctx", None),
            P(("grp", "ctx")),
            P(("grp", "ctx")),
        ),
        out_specs=P(("grp", "ctx"), None),
        check_vma=False,
    )
```

```python
import functools
import math

import jax
import jax.numpy as jnp
import numpy as np
from jax import lax
from jax.experimental import pallas as pl
from jax.experimental.pallas import tpu as pltpu
from jax.sharding import PartitionSpec as P

MESH = pl.DeviceIdType.MESH
F32, BF16 = jnp.float32, jnp.bfloat16
N = 64
GRP = 8


def class_of(dev):
    z, x, core = dev // 8, dev // 2 % 4, dev % 2
    return (x + x // 2) % 2 * 2 + core, x // 2 * 8 + z


def source_of(dev, rank):
    x, core = dev // 2 % 4, dev % 2
    parity = (x + x // 2) % 2
    return (rank % 8 * 4 + parity + rank // 8 * (3 - 2 * parity)) * 2 + core


def holder_of(group, expert):
    parity, core, pair = group // 2, group % 2, expert % 2
    return (expert // 2 * 4 + 2 * pair + (parity + pair) % 2) * 2 + core


def split(table):
    high = table.astype(np.float32).astype(BF16)
    low = (table - high.astype(np.float64)).astype(np.float32).astype(BF16)
    return high, low


@functools.lru_cache(None)
def tables():
    place = np.arange(N)
    parity, core, rank = place // 32, place // 16 % 2, place % 16
    order = (rank % 8 * 4 + parity + rank // 8 * (3 - 2 * parity)) * 2 + core
    quarter = 4 * np.arange(64) + 1
    lane = np.arange(128)

    def angle(first, second, period):
        return 2.0 * math.pi * (np.outer(first, second) % period) / period

    twist = angle(quarter, lane, 32768)
    inner = angle(lane, lane, 128)
    ci, si = np.cos(inner), np.sin(inner)
    out = {"twist": np.stack([np.cos(twist), np.sin(twist)]).astype(np.float32)}
    for name, blocks in (("filt", np.arange(64)), ("sig", order)):
        theta = angle(quarter, blocks, 256)
        high, low = split(np.concatenate([np.cos(theta), -np.sin(theta)], axis=0))
        out["outer_" + name] = np.concatenate([high, low], axis=1)
    theta = angle(order, quarter, 256)
    high, low = split(np.concatenate([np.cos(theta), -np.sin(theta)], axis=1) / 8192.0)
    out["outer_inv"] = np.concatenate([high, low, high], axis=1)
    out["inner"] = np.stack(
        split(np.block([[ci, -si], [si, ci]])) + split(np.block([[ci, si], [-si, ci]])))
    return out


def dot(left, right):
    return jnp.dot(left, right, preferred_element_type=F32)


def halves(value):
    high = value.astype(BF16)
    return high, (value - high.astype(F32)).astype(BF16)


def settle(ref, sem):
    pltpu.make_async_copy(ref, ref, sem).wait()


def kernel(
    tokens, expert_id, slot_index, chan, filt_hbm, gain_ffn, router, w_up, w_down,
    twist, outer_filt, outer_sig, outer_inv, inner_hbm,
    out,
    toks_t, aux, toks, auxes, filt, inner, stage, spec, high, low, diag, packed, rows, mid,
    ffn_in, hidden, out_rows, arrived, up, down,
    s_tok, r_tok, s_aux, r_aux, s_row, r_row, s_out, r_out, s_w, r_w, local,
):
    me = lax.axis_index("ctx")
    grp = lax.axis_index("grp")
    group, my_rank = class_of(me)
    place = group * 16 + my_rank
    expert = me // 4
    partner = me // 2 * 2 + 1 - me % 2
    across = me // 4 * 4 + (me + 2) % 4
    ahead, behind = lax.rem(grp + 1, GRP), lax.rem(grp + GRP - 1, GRP)
    ahead2, behind2 = lax.rem(grp + 2, GRP), lax.rem(grp + GRP - 2, GRP)

    barrier = pltpu.get_barrier_semaphore()

    def greet(i, carry):
        pl.semaphore_signal(
            barrier, inc=1, device_id={"ctx": lax.rem(me + i, N)}, device_id_type=MESH)
        return carry

    lax.fori_loop(1, N, greet, 0)
    for neighbour in (ahead, behind, ahead2, behind2):
        pl.semaphore_signal(barrier, inc=1, device_id={"grp": neighbour}, device_id_type=MESH)

    fetches = [
        pltpu.make_async_copy(filt_hbm, filt, local.at[0]),
        pltpu.make_async_copy(inner_hbm, inner, local.at[1]),
        pltpu.make_async_copy(w_up, up.at[0], local.at[2]),
        pltpu.make_async_copy(w_down, down.at[pl.ds(0, 256)], local.at[3]),
    ]
    for fetch in fetches:
        fetch.start()

    total = jnp.zeros((1, 128), F32)
    for j in range(16):
        block = tokens[:, 128 * j : 128 * j + 128].astype(F32).T
        total = total + jnp.sum(block * block, axis=0, keepdims=True)
        toks_t[4 * j : 4 * j + 4] = block.astype(BF16).reshape(4, 32, 128)
    target = (expert_id[...] * 16 + slot_index[...]).astype(F32)
    aux[0:1, :] = lax.rsqrt(total * (1.0 / 2048.0) + 1e-06)
    aux[1:2, :] = target
    pl.semaphore_wait(barrier, N + 3)

    def push(source, dest, sem, device):
        pltpu.make_async_remote_copy(
            source, dest, s_w.at[sem], r_w.at[sem], device_id=device, device_id_type=MESH
        ).start()

    quarter = lax.rem(grp, 4)
    up_at = pl.multiple_of(quarter * 512, 512)
    down_at = pl.multiple_of(quarter * 64, 64)

    def held_up(first, count):
        return up.at[2, pl.ds(up_at + first, count)]

    def held_down(first, count):
        return down.at[pl.ds(512 + down_at + first, count)]

    push(w_up.at[pl.ds(up_at, 512)], held_up(0, 512), 0, {"ctx": across})
    push(w_down.at[pl.ds(down_at, 64)], held_down(0, 64), 1, {"ctx": across})

    def send_toks(half):
        def send(i, carry):
            peer = lax.rem(me + i, N)
            if half == 0:
                pltpu.make_async_remote_copy(
                    aux, auxes.at[place], s_aux, r_aux, device_id={"ctx": peer},
                    device_id_type=MESH).start()
            channels = pl.ds(16 * half, 16)
            pltpu.make_async_remote_copy(
                toks_t.at[peer, channels], toks.at[place, channels], s_tok.at[half],
                r_tok.at[half], device_id={"ctx": peer}, device_id_type=MESH).start()
            return carry

        lax.fori_loop(1, N, send, 0)

    send_toks(0)
    send_toks(1)
    push(w_up, up.at[1], 2, {"ctx": partner})
    push(w_down, down.at[pl.ds(256, 256)], 3, {"ctx": partner})
    toks[pl.ds(place, 1)] = toks_t[pl.ds(me, 1)]
    auxes[pl.ds(place, 1)] = aux[...].reshape(1, 2, 128)

    def transform(outer, begin, end):
        def channels(i, carry):
            for j in range(4):
                at = pl.multiple_of((4 * i + j) * 64, 64)
                block = stage[pl.ds(at, 64), :].astype(BF16)
                first = dot(outer[...], jnp.concatenate([block, block], axis=0))
                re, im = first[:64], first[64:]
                ct, st = twist[0], twist[1]
                re_h, re_l = halves(re * ct + im * st)
                im_h, im_l = halves(im * ct - re * st)
                high[pl.ds(at, 64), 0:128] = re_h
                high[pl.ds(at, 64), 128:256] = im_h
                low[pl.ds(at, 64), 0:128] = re_l
                low[pl.ds(at, 64), 128:256] = im_l
            return carry

        lax.fori_loop(begin, end, channels, 0)

    def inner_dot(hi, lo, which):
        return dot(hi, inner[which]) + dot(hi, inner[which + 1]) + dot(lo, inner[which])

    def load_filter(i, carry):
        stage[pl.ds(i, 32, stride=64), :] = filt[
            :, pl.ds(pl.multiple_of(i * 128, 128), 128)].astype(F32)
        return carry

    fetches[0].wait()
    fetches[1].wait()
    lax.fori_loop(0, N, load_filter, 0)
    transform(outer_filt, 0, 8)

    def filter_inner(i, carry):
        at = pl.ds(pl.multiple_of(i * 512, 512), 512)
        spec[at, :] = inner_dot(high[at, :], low[at, :], 0)
        return carry

    lax.fori_loop(0, 4, filter_inner, 0)

    settle(held_up(0, 512), r_w.at[0])
    settle(held_down(0, 64), r_w.at[1])
    for first, device in ((0, ahead2), (1, behind2)):
        push(held_up(256 * first, 256), held_up(256 * first, 256), 4, {"grp": device})
        push(held_down(32 * first, 32), held_down(32 * first, 32), 5, {"grp": device})
    for device in (ahead, behind):
        push(held_up(0, 512), held_up(0, 512), 4, {"grp": device})
        push(held_down(0, 64), held_down(0, 64), 5, {"grp": device})

    def convolve(i, carry):
        at = pl.ds(pl.multiple_of(i * 512, 512), 512)
        sig = inner_dot(high[at, :], low[at, :], 0)
        fil = spec[at, :]
        s_re, s_im = sig[:, :128], sig[:, 128:]
        f_re, f_im = fil[:, :128], fil[:, 128:]
        prod = jnp.concatenate([s_re * f_re - s_im * f_im, s_re * f_im + s_im * f_re], axis=1)
        p_h, p_l = halves(prod)
        back = inner_dot(p_h, p_l, 2)
        for j in range(8):
            re, im = back[64 * j : 64 * j + 64, :128], back[64 * j : 64 * j + 64, 128:]
            ct, st = twist[0], twist[1]
            t_h, t_l = halves(jnp.concatenate([re * ct - im * st, im * ct + re * st], axis=0))
            stage[pl.ds(pl.multiple_of(i * 512 + 64 * j, 64), 64), :] = dot(
                outer_inv[...], jnp.concatenate([t_h, t_h, t_l], axis=0))
        return carry

    settle(auxes.at[pl.ds(0, N - 1)], r_aux)
    for half in range(2):
        begin = 16 * half
        settle(toks.at[pl.ds(0, N - 1), pl.ds(begin, 16)], r_tok.at[half])

        def load_signal(i, carry):
            tok = toks[i, begin : begin + 16].astype(F32)
            normed = (tok * auxes[i, 0:1, :] * chan[0, begin : begin + 16]).astype(BF16)
            stage[pl.ds(64 * begin + i, 16, stride=64), :] = normed.astype(F32)
            return carry

        lax.fori_loop(0, N, load_signal, 0)
        transform(outer_sig, 4 * half, 4 * half + 4)
        lax.fori_loop(2 * half, 2 * half + 2, convolve, 0)

    diag[...] = jnp.zeros_like(diag)
    slot_ids = lax.broadcasted_iota(jnp.int32, (256, 128), 0).astype(F32)

    def pack(cls, part):
        picks = []
        for j in range(4):
            idx = cls * 16 + part * 4 + j
            tok = toks[idx].astype(F32)
            normed = (tok * auxes[idx, 0:1, :] * chan[0]).astype(BF16).astype(F32)
            conv = stage[pl.ds(idx, 32, stride=64), :]
            conv_out = (conv + chan[1] * normed).astype(BF16).astype(F32)
            diag[32 * j : 32 * j + 32, 128 * j : 128 * j + 128] = (tok + conv_out).astype(BF16)
            picks.append(jnp.where(slot_ids == auxes[idx, 1:2, :], 1.0, 0.0).astype(BF16))
        picked = lax.dot_general(
            jnp.concatenate(picks, axis=1), diag[...], (((1,), (1,)), ((), ())),
            preferred_element_type=F32)
        packed[cls, :, 16 * part : 16 * part + 16, :] = picked.astype(BF16).reshape(16, 16, 128)

    for half in range(2):

        def pack_class(i, carry):
            cls = lax.rem(group + i, 4)
            pack(cls, 2 * half)
            pack(cls, 2 * half + 1)
            part = pl.ds(32 * half, 32)

            def send(t, carry):
                to = lax.rem(expert + t, 16)
                dest = holder_of(cls, to)

                @pl.when(dest != me)
                def _():
                    pltpu.make_async_remote_copy(
                        packed.at[cls, to, part], rows.at[me, part], s_row.at[half],
                        r_row.at[half], device_id={"ctx": dest}, device_id_type=MESH).start()
                return carry

            lax.fori_loop(0, 16, send, 0)
            return carry

        lax.fori_loop(0, 4, pack_class, 0)

    rows[pl.ds(me, 1)] = packed[group, pl.ds(expert, 1)]

    settle(up.at[2, pl.ds(0, 1536)], r_w.at[4])
    settle(down.at[pl.ds(512, 192)], r_w.at[5])
    push(up.at[2], up.at[3], 6, {"ctx": partner})
    push(down.at[pl.ds(512, 256)], down.at[pl.ds(768, 256)], 7, {"ctx": partner})

    lane = lax.broadcasted_iota(jnp.int32, (16, 128), 1)
    in_half, in_quarter = lane < 64, lane % 64 < 32
    for half in range(2):
        part = pl.ds(32 * half, 32)
        these = pl.ds(128 * half, 128)
        settle(rows.at[pl.ds(0, N - 1), part], r_row.at[half])

        def unpack(i, carry):
            at = pl.ds(pl.multiple_of(i * 128, 128), 128)
            for r in (2 * half, 2 * half + 1):
                v = [rows[4 * i + j, 16 * r : 16 * r + 16, :].astype(F32) for j in range(4)]
                a0 = jnp.where(in_half, v[0], pltpu.roll(v[2], 64, 1))
                a1 = jnp.where(in_half, v[1], pltpu.roll(v[3], 64, 1))
                a2 = jnp.where(in_half, pltpu.roll(v[0], 64, 1), v[2])
                a3 = jnp.where(in_half, pltpu.roll(v[1], 64, 1), v[3])
                u = [
                    jnp.where(in_quarter, a0, pltpu.roll(a1, 32, 1)),
                    jnp.where(in_quarter, pltpu.roll(a0, 96, 1), a1),
                    jnp.where(in_quarter, a2, pltpu.roll(a3, 32, 1)),
                    jnp.where(in_quarter, pltpu.roll(a2, 96, 1), a3),
                ]
                for p in range(4):
                    mid[64 * r + 16 * p : 64 * r + 16 * p + 16, at] = u[p]
            return carry

        lax.fori_loop(0, 16, unpack, 0)

        def norm_rows(i, carry):
            at = pl.ds(pl.multiple_of(i * 32, 32), 32)
            block = mid[at, :]
            scale = lax.rsqrt(
                jnp.sum(block * block, axis=1, keepdims=True) * (1.0 / 2048.0) + 1e-06)
            ffn_in[at, :] = (block * scale * gain_ffn[...]).astype(BF16)
            return carry

        lax.fori_loop(4 * half, 4 * half + 4, norm_rows, 0)
        logits = lax.dot_general(
            ffn_in[these, :], router[...], (((1,), (1,)), ((), ())), preferred_element_type=F32)
        chosen = lax.broadcasted_iota(jnp.int32, logits.shape, 1) == expert
        gate = jax.nn.sigmoid(jnp.sum(jnp.where(chosen, logits, 0.0), axis=1, keepdims=True))

        if half == 0:
            fetches[2].wait()
            fetches[3].wait()
            settle(up.at[1], r_w.at[2])
            settle(down.at[pl.ds(256, 256)], r_w.at[3])
            settle(up.at[3], r_w.at[6])
            settle(down.at[pl.ds(768, 256)], r_w.at[7])

        def go_up(i, carry):
            value = dot(ffn_in[these, :], up[i])
            value = value * (1.0 + lax.erf(value * math.sqrt(0.5))) * 0.5
            hidden[these, pl.ds(pl.multiple_of(i * 256, 256), 256)] = value.astype(BF16)
            return carry

        lax.fori_loop(0, 4, go_up, 0)

        def go_down(i, carry):
            at = pl.ds(pl.multiple_of(i * 256, 256), 256)
            result = dot(hidden[these, :], down[:, at]).astype(BF16).astype(F32)
            value = (mid[these, at] + gate * result).astype(BF16)
            out_rows[8 * half : 8 * half + 8, :, at] = value.reshape(8, 16, 256)
            return carry

        lax.fori_loop(0, 8, go_down, 0)

        def send_out(i, carry):
            rank = 8 * half + lax.rem(my_rank + i, 8)

            @pl.when(rank != my_rank)
            def _():
                pltpu.make_async_remote_copy(
                    out_rows.at[rank], arrived.at[expert], s_out, r_out,
                    device_id={"ctx": source_of(me, rank)}, device_id_type=MESH).start()
            return carry

        lax.fori_loop(0, 8, send_out, 0)

    arrived[pl.ds(expert, 1)] = out_rows[pl.ds(my_rank, 1)]
    pick = jnp.where(slot_ids == target, 1.0, 0.0).T.astype(BF16)
    settle(arrived.at[pl.ds(0, 15)], r_out)

    def select(i, carry):
        at = pl.ds(pl.multiple_of(i * 256, 256), 256)
        out[:, at] = dot(pick, arrived[:, :, at].reshape(256, 256)).astype(BF16)
        return carry

    lax.fori_loop(0, 8, select, 0)

    settle(auxes.at[pl.ds(0, N - 1)], s_aux)
    for half in range(2):
        settle(toks.at[pl.ds(0, N - 1), pl.ds(16 * half, 16)], s_tok.at[half])
        settle(rows.at[pl.ds(0, N - 1), pl.ds(32 * half, 32)], s_row.at[half])
    settle(arrived.at[pl.ds(0, 15)], s_out)
    for sem, ref in enumerate((
        held_up(0, 512), held_down(0, 64), up.at[1], down.at[pl.ds(256, 256)],
        up.at[2, pl.ds(0, 1536)], down.at[pl.ds(512, 192)], up.at[3], down.at[pl.ds(768, 256)],
    )):
        settle(ref, s_w.at[sem])


def body(
    tokens, gain_in, long_filter, skip_gain, gain_ffn, router, w_up, w_down, expert_id, slot_index
):
    me = lax.axis_index("ctx")
    gain = lax.dynamic_slice(gain_in, (me * 32,), (32,))
    chan = jnp.broadcast_to(jnp.stack([gain, skip_gain])[:, :, None], (2, 32, 128))
    t = tables()
    consts = [jnp.asarray(t[k]) for k in ("twist", "outer_filt", "outer_sig", "outer_inv", "inner")]
    vmem = pl.BlockSpec(memory_space=pltpu.VMEM)
    anywhere = pl.BlockSpec(memory_space=pl.ANY)
    dma = pltpu.SemaphoreType.DMA
    return pl.pallas_call(
        kernel,
        out_shape=jax.ShapeDtypeStruct((128, 2048), BF16),
        in_specs=[vmem] * 4 + [anywhere] + [vmem] * 2 + [anywhere] * 2 + [vmem] * 4 + [anywhere],
        out_specs=vmem,
        scratch_shapes=[
            pltpu.VMEM((N, 32, 128), BF16),
            pltpu.VMEM((2, 128), F32),
            pltpu.VMEM((N, 32, 128), BF16),
            pltpu.VMEM((N, 2, 128), F32),
            pltpu.VMEM((32, 8192), BF16),
            pltpu.VMEM((4, 256, 256), BF16),
            pltpu.VMEM((2048, 128), F32),
            pltpu.VMEM((2048, 256), F32),
            pltpu.VMEM((2048, 256), BF16),
            pltpu.VMEM((2048, 256), BF16),
            pltpu.VMEM((128, 512), BF16),
            pltpu.VMEM((4, 16, 64, 128), BF16),
            pltpu.VMEM((N, 64, 128), BF16),
            pltpu.VMEM((256, 2048), F32),
            pltpu.VMEM((256, 2048), BF16),
            pltpu.VMEM((256, 1024), BF16),
            pltpu.VMEM((16, 16, 2048), BF16),
            pltpu.VMEM((16, 16, 2048), BF16),
            pltpu.VMEM((4, 2048, 256), BF16),
            pltpu.VMEM((1024, 2048), BF16),
            dma((2,)), dma((2,)), dma, dma, dma((2,)), dma((2,)), dma, dma, dma((8,)), dma((8,)),
            dma((4,)),
        ],
        compiler_params=pltpu.CompilerParams(
            collective_id=0, has_side_effects=True, vmem_limit_bytes=60 * 1024 * 1024),
    )(
        tokens, expert_id.reshape(1, 128), slot_index.reshape(1, 128), chan, long_filter,
        gain_ffn.reshape(1, 2048), router.T, w_up, w_down, *consts
    )


def solution(mesh):
    return jax.shard_map(
        body,
        mesh=mesh,
        in_specs=(
            P(("grp", "ctx"), None),
            P(),
            P("ctx", None),
            P("ctx"),
            P(),
            P(),
            P(None, "ctx"),
            P("ctx", None),
            P(("grp", "ctx")),
            P(("grp", "ctx")),
        ),
        out_specs=P(("grp", "ctx"), None),
        check_vma=False,
    )
```

```python
import functools
import math

import jax
import jax.numpy as jnp
import numpy as np
from jax import lax
from jax.experimental import pallas as pl
from jax.experimental.pallas import tpu as pltpu
from jax.sharding import PartitionSpec as P

MESH = pl.DeviceIdType.MESH
F32, BF16 = jnp.float32, jnp.bfloat16
N = 64
GRP = 8
PARTS = 2
WIDE = 32 // PARTS


def class_of(dev):
    z, x, core = dev // 8, dev // 2 % 4, dev % 2
    return (x + x // 2) % 2 * 2 + core, (x // 2 + z) % 2 * 8 + z


def source_of(dev, rank):
    x, core = dev // 2 % 4, dev % 2
    parity = (x + x // 2) % 2
    side = (rank // 8 + rank) % 2
    return (rank % 8 * 4 + parity + side * (3 - 2 * parity)) * 2 + core


def holder_of(group, expert):
    parity, core, pair = group // 2, group % 2, expert % 2
    return (expert // 2 * 4 + 2 * pair + (parity + pair) % 2) * 2 + core


def split(table):
    high = table.astype(np.float32).astype(BF16)
    low = (table - high.astype(np.float64)).astype(np.float32).astype(BF16)
    return high, low


@functools.lru_cache(None)
def tables():
    place = np.arange(N)
    parity, core, rank = place // 32, place // 16 % 2, place % 16
    side = (rank // 8 + rank) % 2
    order = (rank % 8 * 4 + parity + side * (3 - 2 * parity)) * 2 + core
    quarter = 4 * np.arange(64) + 1
    lane = np.arange(128)

    def angle(first, second, period):
        return 2.0 * math.pi * (np.outer(first, second) % period) / period

    twist = angle(quarter, lane, 32768)
    inner = angle(lane, lane, 128)
    ci, si = np.cos(inner), np.sin(inner)
    out = {"twist": np.stack([np.cos(twist), np.sin(twist)]).astype(np.float32)}
    for name, blocks in (("filt", np.arange(64)), ("sig", order)):
        theta = angle(quarter, blocks, 256)
        high, low = split(np.concatenate([np.cos(theta), -np.sin(theta)], axis=0))
        out["outer_" + name] = np.concatenate([high, low], axis=1)
    theta = angle(order, quarter, 256)
    high, low = split(np.concatenate([np.cos(theta), -np.sin(theta)], axis=1) / 8192.0)
    out["outer_inv"] = np.concatenate([high, low, high], axis=1)
    out["inner"] = np.stack(
        split(np.block([[ci, -si], [si, ci]])) + split(np.block([[ci, si], [-si, ci]])))
    return out


def dot(left, right):
    return jnp.dot(left, right, preferred_element_type=F32)


def halves(value):
    high = value.astype(BF16)
    return high, (value - high.astype(F32)).astype(BF16)


def settle(ref, sem):
    pltpu.make_async_copy(ref, ref, sem).wait()


def kernel(
    tokens, expert_id, slot_index, gain_in, skip_gain, filt_hbm, gain_ffn, router, w_up, w_down,
    twist, outer_filt, outer_sig, outer_inv, inner_hbm,
    out,
    chan, turned_gain, toks_t, aux, toks, scales, targets, filt, inner, stage, spec, high, low, diag, packed, rows, mid,
    ffn_in, hidden, out_rows, arrived, up, down,
    s_tok, r_tok, s_aux, r_aux, s_tgt, r_tgt, s_row, r_row, s_out, r_out, s_w, r_w, local,
):
    me = lax.axis_index("ctx")
    grp = lax.axis_index("grp")
    group, my_rank = class_of(me)
    place = group * 16 + my_rank
    expert = me // 4
    partner = me // 2 * 2 + 1 - me % 2
    across = me // 4 * 4 + (me + 2) % 4
    ahead, behind = lax.rem(grp + 1, GRP), lax.rem(grp + GRP - 1, GRP)
    ahead2, behind2 = lax.rem(grp + 2, GRP), lax.rem(grp + GRP - 2, GRP)

    barrier = pltpu.get_barrier_semaphore()

    def greet(i, carry):
        pl.semaphore_signal(
            barrier, inc=1, device_id={"ctx": lax.rem(me + i, N)}, device_id_type=MESH)
        return carry

    lax.fori_loop(1, N, greet, 0)
    for neighbour in (ahead, behind, ahead2, behind2):
        pl.semaphore_signal(barrier, inc=1, device_id={"grp": neighbour}, device_id_type=MESH)

    fetches = [
        pltpu.make_async_copy(filt_hbm, filt, local.at[0]),
        pltpu.make_async_copy(inner_hbm, inner, local.at[1]),
        pltpu.make_async_copy(w_up, up.at[0], local.at[2]),
        pltpu.make_async_copy(w_down, down.at[pl.ds(0, 256)], local.at[3]),
    ]
    for fetch in fetches:
        fetch.start()

    total = jnp.zeros((1, 128), F32)
    for j in range(16):
        block = tokens[:, 128 * j : 128 * j + 128].astype(F32).T
        total = total + jnp.sum(block * block, axis=0, keepdims=True)
        toks_t[4 * j : 4 * j + 4] = block.astype(BF16).reshape(4, 32, 128)
    target = (expert_id[...] * 16 + slot_index[...]).astype(F32)
    aux[0] = lax.rsqrt(total * (1.0 / 2048.0) + 1e-06)
    aux[1] = target
    row = gain_in[pl.ds(me // 4, 1), :]
    turned_gain[...] = jnp.broadcast_to(row, (128, 128)).T
    chan[0] = turned_gain[pl.ds(pl.multiple_of(me % 4 * 32, 32), 32), :]
    chan[1] = jnp.broadcast_to(skip_gain[...], (128, 32)).T
    pl.semaphore_wait(barrier, N + 3)

    def push(source, dest, sem, device):
        pltpu.make_async_remote_copy(
            source, dest, s_w.at[sem], r_w.at[sem], device_id=device, device_id_type=MESH
        ).start()

    quarter = lax.rem(grp, 4)
    up_at = pl.multiple_of(quarter * 512, 512)
    down_at = pl.multiple_of(quarter * 64, 64)

    def held_up(first, count):
        return up.at[2, pl.ds(up_at + first, count)]

    def held_down(first, count):
        return down.at[pl.ds(512 + down_at + first, count)]

    def over_x(piece):
        push(
            w_up.at[pl.ds(up_at + 256 * piece, 256)], held_up(256 * piece, 256), 2 * piece,
            {"ctx": across})
        push(
            w_down.at[pl.ds(down_at + 32 * piece, 32)], held_down(32 * piece, 32),
            2 * piece + 1, {"ctx": across})

    def along_grp(piece):
        settle(held_up(256 * piece, 256), r_w.at[2 * piece])
        settle(held_down(32 * piece, 32), r_w.at[2 * piece + 1])
        for first, device in ((0, ahead2), (1, behind2)):
            some_up = held_up(256 * piece + 128 * first, 128)
            some_down = held_down(32 * piece + 16 * first, 16)
            push(some_up, some_up, 4 + 2 * piece, {"grp": device})
            push(some_down, some_down, 5 + 2 * piece, {"grp": device})
        for device in (ahead, behind):
            some_up, some_down = held_up(256 * piece, 256), held_down(32 * piece, 32)
            push(some_up, some_up, 4 + 2 * piece, {"grp": device})
            push(some_down, some_down, 5 + 2 * piece, {"grp": device})

    def to_partner(piece):
        settle(up.at[2, pl.ds(0, 768)], r_w.at[4 + 2 * piece])
        settle(down.at[pl.ds(512, 96)], r_w.at[5 + 2 * piece])
        for q in range(4):
            rows_at = pl.ds(512 * q + 256 * piece, 256)
            push(up.at[2, rows_at], up.at[3, rows_at], 8, {"ctx": partner})
            first = 64 * q + 32 * piece
            push(
                down.at[pl.ds(512 + first, 32)], down.at[pl.ds(768 + first, 32)], 9,
                {"ctx": partner})

    over_x(0)

    def send_aux(which, dest, s_sem, r_sem):
        def send(i, carry):
            pltpu.make_async_remote_copy(
                aux.at[which], dest.at[place], s_sem, r_sem,
                device_id={"ctx": lax.rem(me + i, N)}, device_id_type=MESH).start()
            return carry

        lax.fori_loop(1, N, send, 0)

    def send_toks(part, carry):
        channels = pl.ds(pl.multiple_of(WIDE * part, WIDE), WIDE)

        def send(i, carry):
            peer = lax.rem(me + i, N)
            pltpu.make_async_remote_copy(
                toks_t.at[peer, channels], toks.at[place, channels], s_tok.at[part],
                r_tok.at[part], device_id={"ctx": peer}, device_id_type=MESH).start()
            return carry

        return lax.fori_loop(1, N, send, carry)

    send_aux(0, scales, s_aux, r_aux)
    lax.fori_loop(0, PARTS, send_toks, 0)
    over_x(1)
    send_aux(1, targets, s_tgt, r_tgt)
    push(w_up, up.at[1], 10, {"ctx": partner})
    push(w_down, down.at[pl.ds(256, 256)], 11, {"ctx": partner})
    toks[pl.ds(place, 1)] = toks_t[pl.ds(me, 1)]
    scales[place] = aux[0]
    targets[place] = aux[1]

    diag[...] = jnp.zeros_like(diag)

    def transform(outer, begin, end):
        def channels(i, carry):
            for j in range(4):
                at = pl.multiple_of((4 * i + j) * 64, 64)
                block = stage[pl.ds(at, 64), :].astype(BF16)
                first = dot(outer[...], jnp.concatenate([block, block], axis=0))
                re, im = first[:64], first[64:]
                ct, st = twist[0], twist[1]
                re_h, re_l = halves(re * ct + im * st)
                im_h, im_l = halves(im * ct - re * st)
                high[pl.ds(at, 64), 0:128] = re_h
                high[pl.ds(at, 64), 128:256] = im_h
                low[pl.ds(at, 64), 0:128] = re_l
                low[pl.ds(at, 64), 128:256] = im_l
            return carry

        lax.fori_loop(begin, end, channels, 0)

    def inner_dot(hi, lo, which):
        return dot(hi, inner[which]) + dot(hi, inner[which + 1]) + dot(lo, inner[which])

    def load_filter(i, carry):
        stage[pl.ds(i, 32, stride=64), :] = filt[
            :, pl.ds(pl.multiple_of(i * 128, 128), 128)].astype(F32)
        return carry

    fetches[0].wait()
    fetches[1].wait()
    lax.fori_loop(0, N, load_filter, 0)
    transform(outer_filt, 0, 8)

    def filter_inner(i, carry):
        at = pl.ds(pl.multiple_of(i * 512, 512), 512)
        spec[at, :] = inner_dot(high[at, :], low[at, :], 0)
        return carry

    lax.fori_loop(0, 4, filter_inner, 0)

    along_grp(0)

    def convolve(i, carry):
        at = pl.ds(pl.multiple_of(i * 512, 512), 512)
        sig = inner_dot(high[at, :], low[at, :], 0)
        fil = spec[at, :]
        s_re, s_im = sig[:, :128], sig[:, 128:]
        f_re, f_im = fil[:, :128], fil[:, 128:]
        prod = jnp.concatenate([s_re * f_re - s_im * f_im, s_re * f_im + s_im * f_re], axis=1)
        p_h, p_l = halves(prod)
        back = inner_dot(p_h, p_l, 2)
        for j in range(8):
            re, im = back[64 * j : 64 * j + 64, :128], back[64 * j : 64 * j + 64, 128:]
            ct, st = twist[0], twist[1]
            t_h, t_l = halves(jnp.concatenate([re * ct - im * st, im * ct + re * st], axis=0))
            stage[pl.ds(pl.multiple_of(i * 512 + 64 * j, 64), 64), :] = dot(
                outer_inv[...], jnp.concatenate([t_h, t_h, t_l], axis=0))
        return carry

    settle(scales.at[pl.ds(0, N - 1)], r_aux)
    for part in range(PARTS):
        begin = WIDE * part
        settle(toks.at[pl.ds(0, N - 1), pl.ds(begin, WIDE)], r_tok.at[part])

        def load_signal(i, carry):
            tok = toks[i, begin : begin + WIDE].astype(F32)
            normed = (tok * scales[i] * chan[0, begin : begin + WIDE]).astype(BF16)
            stage[pl.ds(64 * begin + i, WIDE, stride=64), :] = normed.astype(F32)
            return carry

        lax.fori_loop(0, N, load_signal, 0)
        transform(outer_sig, WIDE // 4 * part, WIDE // 4 * (part + 1))
        lax.fori_loop(WIDE // 8 * part, WIDE // 8 * (part + 1), convolve, 0)

    along_grp(1)

    settle(targets.at[pl.ds(0, N - 1)], r_tgt)
    slot_ids = lax.broadcasted_iota(jnp.int32, (256, 128), 0).astype(F32)

    def pack(cls, part):
        picks = []
        for j in range(4):
            idx = cls * 16 + part * 4 + j
            tok = toks[idx].astype(F32)
            normed = (tok * scales[idx] * chan[0]).astype(BF16).astype(F32)
            conv = stage[pl.ds(idx, 32, stride=64), :]
            conv_out = (conv + chan[1] * normed).astype(BF16).astype(F32)
            diag[32 * j : 32 * j + 32, 128 * j : 128 * j + 128] = (tok + conv_out).astype(BF16)
            picks.append(jnp.where(slot_ids == targets[idx], 1.0, 0.0).astype(BF16))
        picked = lax.dot_general(
            jnp.concatenate(picks, axis=1), diag[...], (((1,), (1,)), ((), ())),
            preferred_element_type=F32)
        packed[cls, :, 16 * part : 16 * part + 16, :] = picked.astype(BF16).reshape(16, 16, 128)

    for half in range(2):

        def pack_class(i, carry):
            cls = lax.rem(group + i, 4)
            pack(cls, 2 * half)
            pack(cls, 2 * half + 1)
            part = pl.ds(32 * half, 32)

            def send(t, carry):
                to = lax.rem(expert + t, 16)
                dest = holder_of(cls, to)

                @pl.when(dest != me)
                def _():
                    pltpu.make_async_remote_copy(
                        packed.at[cls, to, part], rows.at[me, part], s_row.at[half],
                        r_row.at[half], device_id={"ctx": dest}, device_id_type=MESH).start()
                return carry

            lax.fori_loop(0, 16, send, 0)
            return carry

        lax.fori_loop(0, 4, pack_class, 0)
        if half == 0:
            to_partner(0)

    rows[pl.ds(me, 1)] = packed[group, pl.ds(expert, 1)]

    to_partner(1)

    lane = lax.broadcasted_iota(jnp.int32, (16, 128), 1)
    in_half, in_quarter = lane < 64, lane % 64 < 32
    for half in range(2):
        part = pl.ds(32 * half, 32)
        these = pl.ds(128 * half, 128)
        settle(rows.at[pl.ds(0, N - 1), part], r_row.at[half])

        def unpack(i, carry):
            at = pl.ds(pl.multiple_of(i * 128, 128), 128)
            for r in (2 * half, 2 * half + 1):
                v = [rows[4 * i + j, 16 * r : 16 * r + 16, :].astype(F32) for j in range(4)]
                a0 = jnp.where(in_half, v[0], pltpu.roll(v[2], 64, 1))
                a1 = jnp.where(in_half, v[1], pltpu.roll(v[3], 64, 1))
                a2 = jnp.where(in_half, pltpu.roll(v[0], 64, 1), v[2])
                a3 = jnp.where(in_half, pltpu.roll(v[1], 64, 1), v[3])
                u = [
                    jnp.where(in_quarter, a0, pltpu.roll(a1, 32, 1)),
                    jnp.where(in_quarter, pltpu.roll(a0, 96, 1), a1),
                    jnp.where(in_quarter, a2, pltpu.roll(a3, 32, 1)),
                    jnp.where(in_quarter, pltpu.roll(a2, 96, 1), a3),
                ]
                for p in range(4):
                    mid[64 * r + 16 * p : 64 * r + 16 * p + 16, at] = u[p]
            return carry

        lax.fori_loop(0, 16, unpack, 0)

        def norm_rows(i, carry):
            at = pl.ds(pl.multiple_of(i * 32, 32), 32)
            block = mid[at, :]
            scale = lax.rsqrt(
                jnp.sum(block * block, axis=1, keepdims=True) * (1.0 / 2048.0) + 1e-06)
            ffn_in[at, :] = (block * scale * gain_ffn[...]).astype(BF16)
            return carry

        lax.fori_loop(4 * half, 4 * half + 4, norm_rows, 0)
        logits = lax.dot_general(
            ffn_in[these, :], router[...], (((1,), (1,)), ((), ())), preferred_element_type=F32)
        chosen = lax.broadcasted_iota(jnp.int32, logits.shape, 1) == expert
        gate = jax.nn.sigmoid(jnp.sum(jnp.where(chosen, logits, 0.0), axis=1, keepdims=True))

        if half == 0:
            fetches[2].wait()
            fetches[3].wait()
            settle(up.at[1], r_w.at[10])
            settle(down.at[pl.ds(256, 256)], r_w.at[11])
            settle(up.at[3], r_w.at[8])
            settle(down.at[pl.ds(768, 256)], r_w.at[9])

        def go_up(i, carry):
            value = dot(ffn_in[these, :], up[i])
            value = value * (1.0 + lax.erf(value * math.sqrt(0.5))) * 0.5
            hidden[these, pl.ds(pl.multiple_of(i * 256, 256), 256)] = value.astype(BF16)
            return carry

        lax.fori_loop(0, 4, go_up, 0)

        def go_down(i, carry):
            at = pl.ds(pl.multiple_of(i * 256, 256), 256)
            result = dot(hidden[these, :], down[:, at]).astype(BF16).astype(F32)
            value = (mid[these, at] + gate * result).astype(BF16)
            out_rows[8 * half : 8 * half + 8, :, at] = value.reshape(8, 16, 256)
            return carry

        lax.fori_loop(0, 8, go_down, 0)

        def send_out(i, carry):
            rank = 8 * half + lax.rem(my_rank + i, 8)

            @pl.when(rank != my_rank)
            def _():
                pltpu.make_async_remote_copy(
                    out_rows.at[rank], arrived.at[expert], s_out, r_out,
                    device_id={"ctx": source_of(me, rank)}, device_id_type=MESH).start()
            return carry

        lax.fori_loop(0, 8, send_out, 0)

    arrived[pl.ds(expert, 1)] = out_rows[pl.ds(my_rank, 1)]
    pick = jnp.where(slot_ids == target, 1.0, 0.0).T.astype(BF16)
    settle(arrived.at[pl.ds(0, 15)], r_out)

    for i in range(2):
        at = pl.ds(1024 * i, 1024)
        out[:, at] = dot(pick, arrived[:, :, at].reshape(256, 1024)).astype(BF16)

    settle(scales.at[pl.ds(0, N - 1)], s_aux)
    settle(targets.at[pl.ds(0, N - 1)], s_tgt)
    for part in range(PARTS):
        settle(toks.at[pl.ds(0, N - 1), pl.ds(WIDE * part, WIDE)], s_tok.at[part])
    for half in range(2):
        settle(rows.at[pl.ds(0, N - 1), pl.ds(32 * half, 32)], s_row.at[half])
    settle(arrived.at[pl.ds(0, 15)], s_out)
    for sem, ref in enumerate((
        held_up(0, 256), held_down(0, 32), held_up(256, 256), held_down(32, 32),
        up.at[2, pl.ds(0, 768)], down.at[pl.ds(512, 96)], up.at[2, pl.ds(0, 768)],
        down.at[pl.ds(512, 96)], up.at[3], down.at[pl.ds(768, 256)], up.at[1],
        down.at[pl.ds(256, 256)],
    )):
        settle(ref, s_w.at[sem])


def body(
    tokens, gain_in, long_filter, skip_gain, gain_ffn, router, w_up, w_down, expert_id, slot_index
):
    t = tables()
    consts = [jnp.asarray(t[k]) for k in ("twist", "outer_filt", "outer_sig", "outer_inv", "inner")]
    vmem = pl.BlockSpec(memory_space=pltpu.VMEM)
    anywhere = pl.BlockSpec(memory_space=pl.ANY)
    dma = pltpu.SemaphoreType.DMA
    return pl.pallas_call(
        kernel,
        out_shape=jax.ShapeDtypeStruct((128, 2048), BF16),
        in_specs=[vmem] * 5 + [anywhere] + [vmem] * 2 + [anywhere] * 2 + [vmem] * 4 + [anywhere],
        out_specs=vmem,
        scratch_shapes=[
            pltpu.VMEM((2, 32, 128), F32),
            pltpu.VMEM((128, 128), F32),
            pltpu.VMEM((N, 32, 128), BF16),
            pltpu.VMEM((2, 1, 128), F32),
            pltpu.VMEM((N, 32, 128), BF16),
            pltpu.VMEM((N, 1, 128), F32),
            pltpu.VMEM((N, 1, 128), F32),
            pltpu.VMEM((32, 8192), BF16),
            pltpu.VMEM((4, 256, 256), BF16),
            pltpu.VMEM((2048, 128), F32),
            pltpu.VMEM((2048, 256), F32),
            pltpu.VMEM((2048, 256), BF16),
            pltpu.VMEM((2048, 256), BF16),
            pltpu.VMEM((128, 512), BF16),
            pltpu.VMEM((4, 16, 64, 128), BF16),
            pltpu.VMEM((N, 64, 128), BF16),
            pltpu.VMEM((256, 2048), F32),
            pltpu.VMEM((256, 2048), BF16),
            pltpu.VMEM((256, 1024), BF16),
            pltpu.VMEM((16, 16, 2048), BF16),
            pltpu.VMEM((16, 16, 2048), BF16),
            pltpu.VMEM((4, 2048, 256), BF16),
            pltpu.VMEM((1024, 2048), BF16),
            dma((PARTS,)), dma((PARTS,)), dma, dma, dma, dma, dma((2,)), dma((2,)), dma, dma, dma((12,)),
            dma((12,)),
            dma((4,)),
        ],
        compiler_params=pltpu.CompilerParams(
            collective_id=0, has_side_effects=True, vmem_limit_bytes=60 * 1024 * 1024),
    )(
        tokens, expert_id.reshape(1, 128), slot_index.reshape(1, 128),
        gain_in.reshape(16, 128), skip_gain.reshape(1, 32), long_filter,
        gain_ffn.reshape(1, 2048), router.T, w_up, w_down, *consts
    )


def solution(mesh):
    return jax.shard_map(
        body,
        mesh=mesh,
        in_specs=(
            P(("grp", "ctx"), None),
            P(),
            P("ctx", None),
            P("ctx"),
            P(),
            P(),
            P(None, "ctx"),
            P("ctx", None),
            P(("grp", "ctx")),
            P(("grp", "ctx")),
        ),
        out_specs=P(("grp", "ctx"), None),
        check_vma=False,
    )
```

```python
import functools
import math

import jax
import jax.numpy as jnp
import numpy as np
from jax import lax
from jax.experimental import pallas as pl
from jax.experimental.pallas import tpu as pltpu
from jax.sharding import PartitionSpec as P

MESH = pl.DeviceIdType.MESH
F32, BF16 = jnp.float32, jnp.bfloat16
N = 64
GRP = 8
PARTS = 2
WIDE = 32 // PARTS


def class_of(dev):
    z, x, core = dev // 8, dev // 2 % 4, dev % 2
    return (x + x // 2) % 2 * 2 + core, (x // 2 + z) % 2 * 8 + z


def source_of(dev, rank):
    x, core = dev // 2 % 4, dev % 2
    parity = (x + x // 2) % 2
    side = (rank // 8 + rank) % 2
    return (rank % 8 * 4 + parity + side * (3 - 2 * parity)) * 2 + core


def holder_of(group, expert):
    parity, core, pair = group // 2, group % 2, expert % 2
    return (expert // 2 * 4 + 2 * pair + (parity + pair) % 2) * 2 + core


def split(table):
    high = table.astype(np.float32).astype(BF16)
    low = (table - high.astype(np.float64)).astype(np.float32).astype(BF16)
    return high, low


@functools.lru_cache(None)
def tables():
    place = np.arange(N)
    parity, core, rank = place // 32, place // 16 % 2, place % 16
    side = (rank // 8 + rank) % 2
    order = (rank % 8 * 4 + parity + side * (3 - 2 * parity)) * 2 + core
    quarter = 4 * np.arange(64) + 1
    lane = np.arange(128)

    def angle(first, second, period):
        return 2.0 * math.pi * (np.outer(first, second) % period) / period

    twist = angle(quarter, lane, 32768)
    inner = angle(lane, lane, 128)
    ci, si = np.cos(inner), np.sin(inner)
    out = {"twist": np.stack([np.cos(twist), np.sin(twist)]).astype(np.float32)}
    for name, blocks in (("filt", np.arange(64)), ("sig", order)):
        theta = angle(quarter, blocks, 256)
        high, low = split(np.concatenate([np.cos(theta), -np.sin(theta)], axis=0))
        out["outer_" + name] = np.concatenate([high, low], axis=1)
    theta = angle(order, quarter, 256)
    high, low = split(np.concatenate([np.cos(theta), -np.sin(theta)], axis=1) / 8192.0)
    out["outer_inv"] = np.concatenate([high, low, high], axis=1)
    out["inner"] = np.stack(
        split(np.block([[ci, -si], [si, ci]])) + split(np.block([[ci, si], [-si, ci]])))
    return out


def dot(left, right):
    return jnp.dot(left, right, preferred_element_type=F32)


def halves(value):
    high = value.astype(BF16)
    return high, (value - high.astype(F32)).astype(BF16)


def settle(ref, sem):
    pltpu.make_async_copy(ref, ref, sem).wait()


def kernel(
    tokens, expert_id, slot_index, gain_in, skip_gain, filt_hbm, gain_ffn, router, w_up, w_down,
    twist, outer_filt, outer_sig, outer_inv, inner_hbm,
    out,
    chan, turned_gain, toks_t, aux, toks, scales, targets, filt, inner, stage, spec, high, low, diag, packed, rows, mid,
    ffn_in, hidden, out_rows, arrived, up, down,
    s_tok, r_tok, s_aux, r_aux, s_tgt, r_tgt, s_row, r_row, s_out, r_out, s_w, r_w, local,
):
    me = lax.axis_index("ctx")
    grp = lax.axis_index("grp")
    group, my_rank = class_of(me)
    place = group * 16 + my_rank
    expert = me // 4
    partner = me // 2 * 2 + 1 - me % 2
    across = me // 4 * 4 + (me + 2) % 4
    ahead, behind = lax.rem(grp + 1, GRP), lax.rem(grp + GRP - 1, GRP)
    ahead2, behind2 = lax.rem(grp + 2, GRP), lax.rem(grp + GRP - 2, GRP)

    barrier = pltpu.get_barrier_semaphore()

    def greet(i, carry):
        pl.semaphore_signal(
            barrier, inc=1, device_id={"ctx": lax.rem(me + i, N)}, device_id_type=MESH)
        return carry

    lax.fori_loop(1, N, greet, 0, unroll=7)
    for neighbour in (ahead, behind, ahead2, behind2):
        pl.semaphore_signal(barrier, inc=1, device_id={"grp": neighbour}, device_id_type=MESH)

    fetches = [
        pltpu.make_async_copy(filt_hbm, filt, local.at[0]),
        pltpu.make_async_copy(inner_hbm, inner, local.at[1]),
        pltpu.make_async_copy(w_up, up.at[0], local.at[2]),
        pltpu.make_async_copy(w_down, down.at[pl.ds(0, 256)], local.at[3]),
    ]
    for fetch in fetches:
        fetch.start()

    total = jnp.zeros((1, 128), F32)
    for j in range(16):
        block = tokens[:, 128 * j : 128 * j + 128].astype(F32).T
        total = total + jnp.sum(block * block, axis=0, keepdims=True)
        toks_t[4 * j : 4 * j + 4] = block.astype(BF16).reshape(4, 32, 128)
    target = (expert_id[...] * 16 + slot_index[...]).astype(F32)
    aux[0] = lax.rsqrt(total * (1.0 / 2048.0) + 1e-06)
    aux[1] = target
    row = gain_in[pl.ds(me // 4, 1), :]
    turned_gain[...] = jnp.broadcast_to(row, (128, 128)).T
    chan[0] = turned_gain[pl.ds(pl.multiple_of(me % 4 * 32, 32), 32), :]
    chan[1] = jnp.broadcast_to(skip_gain[...], (128, 32)).T
    pl.semaphore_wait(barrier, N + 3)

    def push(source, dest, sem, device):
        pltpu.make_async_remote_copy(
            source, dest, s_w.at[sem], r_w.at[sem], device_id=device, device_id_type=MESH
        ).start()

    quarter = lax.rem(grp, 4)
    up_at = pl.multiple_of(quarter * 512, 512)
    down_at = pl.multiple_of(quarter * 64, 64)

    def held_up(first, count):
        return up.at[2, pl.ds(up_at + first, count)]

    def held_down(first, count):
        return down.at[pl.ds(512 + down_at + first, count)]

    def over_x(piece):
        push(
            w_up.at[pl.ds(up_at + 256 * piece, 256)], held_up(256 * piece, 256), 2 * piece,
            {"ctx": across})
        push(
            w_down.at[pl.ds(down_at + 32 * piece, 32)], held_down(32 * piece, 32),
            2 * piece + 1, {"ctx": across})

    def along_grp(piece):
        settle(held_up(256 * piece, 256), r_w.at[2 * piece])
        settle(held_down(32 * piece, 32), r_w.at[2 * piece + 1])
        for first, device in ((0, ahead2), (1, behind2)):
            some_up = held_up(256 * piece + 128 * first, 128)
            some_down = held_down(32 * piece + 16 * first, 16)
            push(some_up, some_up, 4 + 2 * piece, {"grp": device})
            push(some_down, some_down, 5 + 2 * piece, {"grp": device})
        for device in (ahead, behind):
            some_up, some_down = held_up(256 * piece, 256), held_down(32 * piece, 32)
            push(some_up, some_up, 4 + 2 * piece, {"grp": device})
            push(some_down, some_down, 5 + 2 * piece, {"grp": device})

    def to_partner(piece):
        settle(up.at[2, pl.ds(0, 768)], r_w.at[4 + 2 * piece])
        settle(down.at[pl.ds(512, 96)], r_w.at[5 + 2 * piece])
        for q in range(4):
            rows_at = pl.ds(512 * q + 256 * piece, 256)
            push(up.at[2, rows_at], up.at[3, rows_at], 8, {"ctx": partner})
            first = 64 * q + 32 * piece
            push(
                down.at[pl.ds(512 + first, 32)], down.at[pl.ds(768 + first, 32)], 9,
                {"ctx": partner})

    over_x(0)

    def send_aux(which, dest, s_sem, r_sem):
        def send(i, carry):
            pltpu.make_async_remote_copy(
                aux.at[which], dest.at[place], s_sem, r_sem,
                device_id={"ctx": lax.rem(me + i, N)}, device_id_type=MESH).start()
            return carry

        lax.fori_loop(1, N, send, 0, unroll=7)

    def send_toks(part, carry):
        channels = pl.ds(pl.multiple_of(WIDE * part, WIDE), WIDE)

        def send(i, carry):
            peer = lax.rem(me + i, N)
            pltpu.make_async_remote_copy(
                toks_t.at[peer, channels], toks.at[place, channels], s_tok.at[part],
                r_tok.at[part], device_id={"ctx": peer}, device_id_type=MESH).start()
            return carry

        return lax.fori_loop(1, N, send, carry, unroll=7)

    send_aux(0, scales, s_aux, r_aux)
    lax.fori_loop(0, PARTS, send_toks, 0)
    over_x(1)
    send_aux(1, targets, s_tgt, r_tgt)
    push(w_up, up.at[1], 10, {"ctx": partner})
    push(w_down, down.at[pl.ds(256, 256)], 11, {"ctx": partner})
    toks[pl.ds(place, 1)] = toks_t[pl.ds(me, 1)]
    scales[place] = aux[0]
    targets[place] = aux[1]

    diag[...] = jnp.zeros_like(diag)

    def transform(outer, begin, end):
        def channels(i, carry):
            for j in range(8):
                at = pl.multiple_of((8 * i + j) * 64, 64)
                block = stage[pl.ds(at, 64), :].astype(BF16)
                first = dot(outer[...], jnp.concatenate([block, block], axis=0))
                re, im = first[:64], first[64:]
                ct, st = twist[0], twist[1]
                re_h, re_l = halves(re * ct + im * st)
                im_h, im_l = halves(im * ct - re * st)
                high[pl.ds(at, 64), 0:128] = re_h
                high[pl.ds(at, 64), 128:256] = im_h
                low[pl.ds(at, 64), 0:128] = re_l
                low[pl.ds(at, 64), 128:256] = im_l
            return carry

        lax.fori_loop(begin, end, channels, 0)

    def inner_dot(hi, lo, which):
        return dot(hi, inner[which]) + dot(hi, inner[which + 1]) + dot(lo, inner[which])

    def load_filter(i, carry):
        stage[pl.ds(i, 32, stride=64), :] = filt[
            :, pl.ds(pl.multiple_of(i * 128, 128), 128)].astype(F32)
        return carry

    fetches[0].wait()
    fetches[1].wait()
    lax.fori_loop(0, N, load_filter, 0, unroll=4)
    transform(outer_filt, 0, 4)

    def filter_inner(i, carry):
        at = pl.ds(pl.multiple_of(i * 512, 512), 512)
        spec[at, :] = inner_dot(high[at, :], low[at, :], 0)
        return carry

    lax.fori_loop(0, 4, filter_inner, 0, unroll=2)

    along_grp(0)

    def convolve(i, carry):
        at = pl.ds(pl.multiple_of(i * 512, 512), 512)
        sig = inner_dot(high[at, :], low[at, :], 0)
        fil = spec[at, :]
        s_re, s_im = sig[:, :128], sig[:, 128:]
        f_re, f_im = fil[:, :128], fil[:, 128:]
        prod = jnp.concatenate([s_re * f_re - s_im * f_im, s_re * f_im + s_im * f_re], axis=1)
        p_h, p_l = halves(prod)
        back = inner_dot(p_h, p_l, 2)
        for j in range(8):
            re, im = back[64 * j : 64 * j + 64, :128], back[64 * j : 64 * j + 64, 128:]
            ct, st = twist[0], twist[1]
            t_h, t_l = halves(jnp.concatenate([re * ct - im * st, im * ct + re * st], axis=0))
            stage[pl.ds(pl.multiple_of(i * 512 + 64 * j, 64), 64), :] = dot(
                outer_inv[...], jnp.concatenate([t_h, t_h, t_l], axis=0))
        return carry

    settle(scales.at[pl.ds(0, N - 1)], r_aux)
    for part in range(PARTS):
        begin = WIDE * part
        settle(toks.at[pl.ds(0, N - 1), pl.ds(begin, WIDE)], r_tok.at[part])

        def load_signal(i, carry):
            tok = toks[i, begin : begin + WIDE].astype(F32)
            normed = (tok * scales[i] * chan[0, begin : begin + WIDE]).astype(BF16)
            stage[pl.ds(64 * begin + i, WIDE, stride=64), :] = normed.astype(F32)
            return carry

        lax.fori_loop(0, N, load_signal, 0, unroll=4)
        transform(outer_sig, WIDE // 8 * part, WIDE // 8 * (part + 1))
        lax.fori_loop(WIDE // 8 * part, WIDE // 8 * (part + 1), convolve, 0)

    along_grp(1)

    settle(targets.at[pl.ds(0, N - 1)], r_tgt)
    slot_ids = lax.broadcasted_iota(jnp.int32, (256, 128), 0).astype(F32)

    def pack(cls, part):
        picks = []
        for j in range(4):
            idx = cls * 16 + part * 4 + j
            tok = toks[idx].astype(F32)
            normed = (tok * scales[idx] * chan[0]).astype(BF16).astype(F32)
            conv = stage[pl.ds(idx, 32, stride=64), :]
            conv_out = (conv + chan[1] * normed).astype(BF16).astype(F32)
            diag[32 * j : 32 * j + 32, 128 * j : 128 * j + 128] = (tok + conv_out).astype(BF16)
            picks.append(jnp.where(slot_ids == targets[idx], 1.0, 0.0).astype(BF16))
        picked = lax.dot_general(
            jnp.concatenate(picks, axis=1), diag[...], (((1,), (1,)), ((), ())),
            preferred_element_type=F32)
        packed[cls, :, 16 * part : 16 * part + 16, :] = picked.astype(BF16).reshape(16, 16, 128)

    for half in range(2):

        def pack_class(i, carry):
            cls = lax.rem(group + i, 4)
            pack(cls, 2 * half)
            pack(cls, 2 * half + 1)
            part = pl.ds(32 * half, 32)

            def send(t, carry):
                to = lax.rem(expert + t, 16)
                dest = holder_of(cls, to)

                @pl.when(dest != me)
                def _():
                    pltpu.make_async_remote_copy(
                        packed.at[cls, to, part], rows.at[me, part], s_row.at[half],
                        r_row.at[half], device_id={"ctx": dest}, device_id_type=MESH).start()
                return carry

            lax.fori_loop(0, 16, send, 0)
            return carry

        lax.fori_loop(0, 4, pack_class, 0)
        if half == 0:
            to_partner(0)

    rows[pl.ds(me, 1)] = packed[group, pl.ds(expert, 1)]

    to_partner(1)

    lane = lax.broadcasted_iota(jnp.int32, (16, 128), 1)
    in_half, in_quarter = lane < 64, lane % 64 < 32
    for half in range(2):
        part = pl.ds(32 * half, 32)
        these = pl.ds(128 * half, 128)
        settle(rows.at[pl.ds(0, N - 1), part], r_row.at[half])

        def unpack(i, carry):
            at = pl.ds(pl.multiple_of(i * 128, 128), 128)
            for r in (2 * half, 2 * half + 1):
                v = [rows[4 * i + j, 16 * r : 16 * r + 16, :].astype(F32) for j in range(4)]
                a0 = jnp.where(in_half, v[0], pltpu.roll(v[2], 64, 1))
                a1 = jnp.where(in_half, v[1], pltpu.roll(v[3], 64, 1))
                a2 = jnp.where(in_half, pltpu.roll(v[0], 64, 1), v[2])
                a3 = jnp.where(in_half, pltpu.roll(v[1], 64, 1), v[3])
                u = [
                    jnp.where(in_quarter, a0, pltpu.roll(a1, 32, 1)),
                    jnp.where(in_quarter, pltpu.roll(a0, 96, 1), a1),
                    jnp.where(in_quarter, a2, pltpu.roll(a3, 32, 1)),
                    jnp.where(in_quarter, pltpu.roll(a2, 96, 1), a3),
                ]
                for p in range(4):
                    mid[64 * r + 16 * p : 64 * r + 16 * p + 16, at] = u[p]
            return carry

        lax.fori_loop(0, 16, unpack, 0, unroll=2)

        def norm_rows(i, carry):
            at = pl.ds(pl.multiple_of(i * 32, 32), 32)
            block = mid[at, :]
            scale = lax.rsqrt(
                jnp.sum(block * block, axis=1, keepdims=True) * (1.0 / 2048.0) + 1e-06)
            ffn_in[at, :] = (block * scale * gain_ffn[...]).astype(BF16)
            return carry

        lax.fori_loop(4 * half, 4 * half + 4, norm_rows, 0, unroll=2)
        logits = lax.dot_general(
            ffn_in[these, :], router[...], (((1,), (1,)), ((), ())), preferred_element_type=F32)
        chosen = lax.broadcasted_iota(jnp.int32, logits.shape, 1) == expert
        gate = jax.nn.sigmoid(jnp.sum(jnp.where(chosen, logits, 0.0), axis=1, keepdims=True))

        if half == 0:
            fetches[2].wait()
            fetches[3].wait()
            settle(up.at[1], r_w.at[10])
            settle(down.at[pl.ds(256, 256)], r_w.at[11])
            settle(up.at[3], r_w.at[8])
            settle(down.at[pl.ds(768, 256)], r_w.at[9])

        def go_up(i, carry):
            value = dot(ffn_in[these, :], up[i])
            value = value * (1.0 + lax.erf(value * math.sqrt(0.5))) * 0.5
            hidden[these, pl.ds(pl.multiple_of(i * 256, 256), 256)] = value.astype(BF16)
            return carry

        lax.fori_loop(0, 4, go_up, 0, unroll=2)

        def go_down(i, carry):
            at = pl.ds(pl.multiple_of(i * 256, 256), 256)
            result = dot(hidden[these, :], down[:, at]).astype(BF16).astype(F32)
            value = (mid[these, at] + gate * result).astype(BF16)
            out_rows[8 * half : 8 * half + 8, :, at] = value.reshape(8, 16, 256)
            return carry

        lax.fori_loop(0, 8, go_down, 0, unroll=2)

        def send_out(i, carry):
            rank = 8 * half + lax.rem(my_rank + i, 8)

            @pl.when(rank != my_rank)
            def _():
                pltpu.make_async_remote_copy(
                    out_rows.at[rank], arrived.at[expert], s_out, r_out,
                    device_id={"ctx": source_of(me, rank)}, device_id_type=MESH).start()
            return carry

        lax.fori_loop(0, 8, send_out, 0)

    arrived[pl.ds(expert, 1)] = out_rows[pl.ds(my_rank, 1)]
    pick = jnp.where(slot_ids == target, 1.0, 0.0).T.astype(BF16)
    settle(arrived.at[pl.ds(0, 15)], r_out)

    for i in range(2):
        at = pl.ds(1024 * i, 1024)
        out[:, at] = dot(pick, arrived[:, :, at].reshape(256, 1024)).astype(BF16)

    settle(scales.at[pl.ds(0, N - 1)], s_aux)
    settle(targets.at[pl.ds(0, N - 1)], s_tgt)
    for part in range(PARTS):
        settle(toks.at[pl.ds(0, N - 1), pl.ds(WIDE * part, WIDE)], s_tok.at[part])
    for half in range(2):
        settle(rows.at[pl.ds(0, N - 1), pl.ds(32 * half, 32)], s_row.at[half])
    settle(arrived.at[pl.ds(0, 15)], s_out)
    for sem, ref in enumerate((
        held_up(0, 256), held_down(0, 32), held_up(256, 256), held_down(32, 32),
        up.at[2, pl.ds(0, 768)], down.at[pl.ds(512, 96)], up.at[2, pl.ds(0, 768)],
        down.at[pl.ds(512, 96)], up.at[3], down.at[pl.ds(768, 256)], up.at[1],
        down.at[pl.ds(256, 256)],
    )):
        settle(ref, s_w.at[sem])


def body(
    tokens, gain_in, long_filter, skip_gain, gain_ffn, router, w_up, w_down, expert_id, slot_index
):
    t = tables()
    consts = [jnp.asarray(t[k]) for k in ("twist", "outer_filt", "outer_sig", "outer_inv", "inner")]
    vmem = pl.BlockSpec(memory_space=pltpu.VMEM)
    anywhere = pl.BlockSpec(memory_space=pl.ANY)
    dma = pltpu.SemaphoreType.DMA
    return pl.pallas_call(
        kernel,
        out_shape=jax.ShapeDtypeStruct((128, 2048), BF16),
        in_specs=[vmem] * 5 + [anywhere] + [vmem] * 2 + [anywhere] * 2 + [vmem] * 4 + [anywhere],
        out_specs=vmem,
        scratch_shapes=[
            pltpu.VMEM((2, 32, 128), F32),
            pltpu.VMEM((128, 128), F32),
            pltpu.VMEM((N, 32, 128), BF16),
            pltpu.VMEM((2, 1, 128), F32),
            pltpu.VMEM((N, 32, 128), BF16),
            pltpu.VMEM((N, 1, 128), F32),
            pltpu.VMEM((N, 1, 128), F32),
            pltpu.VMEM((32, 8192), BF16),
            pltpu.VMEM((4, 256, 256), BF16),
            pltpu.VMEM((2048, 128), F32),
            pltpu.VMEM((2048, 256), F32),
            pltpu.VMEM((2048, 256), BF16),
            pltpu.VMEM((2048, 256), BF16),
            pltpu.VMEM((128, 512), BF16),
            pltpu.VMEM((4, 16, 64, 128), BF16),
            pltpu.VMEM((N, 64, 128), BF16),
            pltpu.VMEM((256, 2048), F32),
            pltpu.VMEM((256, 2048), BF16),
            pltpu.VMEM((256, 1024), BF16),
            pltpu.VMEM((16, 16, 2048), BF16),
            pltpu.VMEM((16, 16, 2048), BF16),
            pltpu.VMEM((4, 2048, 256), BF16),
            pltpu.VMEM((1024, 2048), BF16),
            dma((PARTS,)), dma((PARTS,)), dma, dma, dma, dma, dma((2,)), dma((2,)), dma, dma, dma((12,)),
            dma((12,)),
            dma((4,)),
        ],
        compiler_params=pltpu.CompilerParams(
            collective_id=0, has_side_effects=True, vmem_limit_bytes=60 * 1024 * 1024),
    )(
        tokens, expert_id.reshape(1, 128), slot_index.reshape(1, 128),
        gain_in.reshape(16, 128), skip_gain.reshape(1, 32), long_filter,
        gain_ffn.reshape(1, 2048), router.T, w_up, w_down, *consts
    )


def solution(mesh):
    return jax.shard_map(
        body,
        mesh=mesh,
        in_specs=(
            P(("grp", "ctx"), None),
            P(),
            P("ctx", None),
            P("ctx"),
            P(),
            P(),
            P(None, "ctx"),
            P("ctx", None),
            P(("grp", "ctx")),
            P(("grp", "ctx")),
        ),
        out_specs=P(("grp", "ctx"), None),
        check_vma=False,
    )
```

```python
import functools
import math

import jax
import jax.numpy as jnp
import numpy as np
from jax import lax
from jax.experimental import pallas as pl
from jax.experimental.pallas import tpu as pltpu
from jax.sharding import PartitionSpec as P

MESH = pl.DeviceIdType.MESH
F32, BF16 = jnp.float32, jnp.bfloat16
N = 64
GRP = 8
PARTS = 2
WIDE = 32 // PARTS


def class_of(dev):
    z, x, core = dev // 8, dev // 2 % 4, dev % 2
    return (x + x // 2) % 2 * 2 + core, (x // 2 + z) % 2 * 8 + z


def source_of(dev, rank):
    x, core = dev // 2 % 4, dev % 2
    parity = (x + x // 2) % 2
    side = (rank // 8 + rank) % 2
    return (rank % 8 * 4 + parity + side * (3 - 2 * parity)) * 2 + core


def holder_of(group, expert):
    parity, core, pair = group // 2, group % 2, expert % 2
    return (expert // 2 * 4 + 2 * pair + (parity + pair) % 2) * 2 + core


def split(table):
    high = table.astype(np.float32).astype(BF16)
    low = (table - high.astype(np.float64)).astype(np.float32).astype(BF16)
    return high, low


@functools.lru_cache(None)
def tables():
    place = np.arange(N)
    parity, core, rank = place // 32, place // 16 % 2, place % 16
    side = (rank // 8 + rank) % 2
    order = (rank % 8 * 4 + parity + side * (3 - 2 * parity)) * 2 + core
    quarter = 4 * np.arange(64) + 1
    lane = np.arange(128)

    def angle(first, second, period):
        return 2.0 * math.pi * (np.outer(first, second) % period) / period

    twist = angle(quarter, lane, 32768)
    inner = angle(lane, lane, 128)
    ci, si = np.cos(inner), np.sin(inner)
    out = {"twist": np.stack([np.cos(twist), np.sin(twist)]).astype(np.float32)}
    for name, blocks in (("filt", np.arange(64)), ("sig", order)):
        theta = angle(quarter, blocks, 256)
        high, low = split(np.concatenate([np.cos(theta), -np.sin(theta)], axis=0))
        out["outer_" + name] = np.concatenate([high, low], axis=1)
    theta = angle(order, quarter, 256)
    high, low = split(np.concatenate([np.cos(theta), -np.sin(theta)], axis=1) / 8192.0)
    out["outer_inv"] = np.concatenate([high, low, high], axis=1)
    out["inner"] = np.stack(
        split(np.block([[ci, -si], [si, ci]])) + split(np.block([[ci, si], [-si, ci]])))
    return out


def dot(left, right):
    return jnp.dot(left, right, preferred_element_type=F32)


def halves(value):
    high = value.astype(BF16)
    return high, (value - high.astype(F32)).astype(BF16)


def settle(ref, sem):
    pltpu.make_async_copy(ref, ref, sem).wait()


def kernel(
    tokens, expert_id, slot_index, gain_in, skip_gain, filt_hbm, gain_ffn, router, w_up, w_down,
    twist, outer_filt, outer_sig, outer_inv, inner_hbm,
    out,
    chan, turned_gain, toks_t, aux, toks, scales, targets, filt, inner, stage, spec, high, low, diag, packed, rows, mid,
    ffn_in, hidden, out_rows, arrived, up, down,
    s_tok, r_tok, s_aux, r_aux, s_tgt, r_tgt, s_row, r_row, s_out, r_out, s_w, r_w, local,
):
    me = lax.axis_index("ctx")
    grp = lax.axis_index("grp")
    group, my_rank = class_of(me)
    place = group * 16 + my_rank
    expert = me // 4
    partner = me // 2 * 2 + 1 - me % 2
    across = me // 4 * 4 + (me + 2) % 4
    ahead, behind = lax.rem(grp + 1, GRP), lax.rem(grp + GRP - 1, GRP)
    ahead2, behind2 = lax.rem(grp + 2, GRP), lax.rem(grp + GRP - 2, GRP)

    barrier = pltpu.get_barrier_semaphore()

    def greet(i, carry):
        pl.semaphore_signal(
            barrier, inc=1, device_id={"ctx": lax.rem(me + i, N)}, device_id_type=MESH)
        return carry

    lax.fori_loop(1, N, greet, 0, unroll=7)
    for neighbour in (ahead, behind, ahead2, behind2):
        pl.semaphore_signal(barrier, inc=1, device_id={"grp": neighbour}, device_id_type=MESH)

    fetches = [
        pltpu.make_async_copy(filt_hbm, filt, local.at[0]),
        pltpu.make_async_copy(inner_hbm, inner, local.at[1]),
        pltpu.make_async_copy(w_up, up.at[0], local.at[2]),
        pltpu.make_async_copy(w_down, down.at[pl.ds(0, 256)], local.at[3]),
    ]
    for fetch in fetches:
        fetch.start()

    total = jnp.zeros((1, 128), F32)
    for j in range(16):
        block = tokens[:, 128 * j : 128 * j + 128].astype(F32).T
        total = total + jnp.sum(block * block, axis=0, keepdims=True)
        toks_t[4 * j : 4 * j + 4] = block.astype(BF16).reshape(4, 32, 128)
    target = (expert_id[...] * 16 + slot_index[...]).astype(F32)
    aux[0] = lax.rsqrt(total * (1.0 / 2048.0) + 1e-06)
    aux[1] = target
    row = gain_in[pl.ds(me // 4, 1), :]
    turned_gain[...] = jnp.broadcast_to(row, (128, 128)).T
    chan[0] = turned_gain[pl.ds(pl.multiple_of(me % 4 * 32, 32), 32), :]
    chan[1] = jnp.broadcast_to(skip_gain[...], (128, 32)).T
    pl.semaphore_wait(barrier, N + 3)

    def push(source, dest, sem, device):
        pltpu.make_async_remote_copy(
            source, dest, s_w.at[sem], r_w.at[sem], device_id=device, device_id_type=MESH
        ).start()

    quarter = lax.rem(grp, 4)
    up_at = pl.multiple_of(quarter * 512, 512)
    down_at = pl.multiple_of(quarter * 64, 64)

    def held_up(first, count):
        return up.at[2, pl.ds(up_at + first, count)]

    def held_down(first, count):
        return down.at[pl.ds(512 + down_at + first, count)]

    def over_x(piece):
        push(
            w_up.at[pl.ds(up_at + 256 * piece, 256)], held_up(256 * piece, 256), 2 * piece,
            {"ctx": across})
        push(
            w_down.at[pl.ds(down_at + 32 * piece, 32)], held_down(32 * piece, 32),
            2 * piece + 1, {"ctx": across})

    def along_grp(piece):
        settle(held_up(256 * piece, 256), r_w.at[2 * piece])
        settle(held_down(32 * piece, 32), r_w.at[2 * piece + 1])
        for first, device in ((0, ahead2), (1, behind2)):
            some_up = held_up(256 * piece + 128 * first, 128)
            some_down = held_down(32 * piece + 16 * first, 16)
            push(some_up, some_up, 4 + 2 * piece, {"grp": device})
            push(some_down, some_down, 5 + 2 * piece, {"grp": device})
        for device in (ahead, behind):
            some_up, some_down = held_up(256 * piece, 256), held_down(32 * piece, 32)
            push(some_up, some_up, 4 + 2 * piece, {"grp": device})
            push(some_down, some_down, 5 + 2 * piece, {"grp": device})

    def to_partner(piece):
        settle(up.at[2, pl.ds(0, 768)], r_w.at[4 + 2 * piece])
        settle(down.at[pl.ds(512, 96)], r_w.at[5 + 2 * piece])
        for q in range(4):
            rows_at = pl.ds(512 * q + 256 * piece, 256)
            push(up.at[2, rows_at], up.at[3, rows_at], 8, {"ctx": partner})
            first = 64 * q + 32 * piece
            push(
                down.at[pl.ds(512 + first, 32)], down.at[pl.ds(768 + first, 32)], 9,
                {"ctx": partner})

    over_x(0)

    def send_aux(which, dest, s_sem, r_sem):
        def send(i, carry):
            pltpu.make_async_remote_copy(
                aux.at[which], dest.at[place], s_sem, r_sem,
                device_id={"ctx": lax.rem(me + i, N)}, device_id_type=MESH).start()
            return carry

        lax.fori_loop(1, N, send, 0, unroll=7)

    def send_toks(part, carry):
        channels = pl.ds(pl.multiple_of(WIDE * part, WIDE), WIDE)

        def send(i, carry):
            peer = lax.rem(me + i, N)
            pltpu.make_async_remote_copy(
                toks_t.at[peer, channels], toks.at[place, channels], s_tok.at[part],
                r_tok.at[part], device_id={"ctx": peer}, device_id_type=MESH).start()
            return carry

        return lax.fori_loop(1, N, send, carry, unroll=7)

    send_aux(0, scales, s_aux, r_aux)
    lax.fori_loop(0, PARTS, send_toks, 0)
    over_x(1)
    send_aux(1, targets, s_tgt, r_tgt)
    push(w_up, up.at[1], 10, {"ctx": partner})
    push(w_down, down.at[pl.ds(256, 256)], 11, {"ctx": partner})
    toks[pl.ds(place, 1)] = toks_t[pl.ds(me, 1)]
    scales[place] = aux[0]
    targets[place] = aux[1]

    diag[...] = jnp.zeros_like(diag)

    def transform(outer, begin, end):
        def channels(i, carry):
            for j in range(8):
                at = pl.multiple_of((8 * i + j) * 64, 64)
                block = stage[pl.ds(at, 64), :].astype(BF16)
                first = dot(outer[...], jnp.concatenate([block, block], axis=0))
                re, im = first[:64], first[64:]
                ct, st = twist[0], twist[1]
                re_h, re_l = halves(re * ct + im * st)
                im_h, im_l = halves(im * ct - re * st)
                high[pl.ds(at, 64), 0:128] = re_h
                high[pl.ds(at, 64), 128:256] = im_h
                low[pl.ds(at, 64), 0:128] = re_l
                low[pl.ds(at, 64), 128:256] = im_l
            return carry

        lax.fori_loop(begin, end, channels, 0)

    def inner_dot(hi, lo, which):
        return dot(hi, inner[which]) + dot(hi, inner[which + 1]) + dot(lo, inner[which])

    def load_filter(i, carry):
        stage[pl.ds(i, 32, stride=64), :] = filt[
            :, pl.ds(pl.multiple_of(i * 128, 128), 128)].astype(F32)
        return carry

    fetches[0].wait()
    fetches[1].wait()
    lax.fori_loop(0, N, load_filter, 0, unroll=4)
    transform(outer_filt, 0, 4)

    def filter_inner(i, carry):
        at = pl.ds(pl.multiple_of(i * 512, 512), 512)
        spec[at, :] = inner_dot(high[at, :], low[at, :], 0)
        return carry

    lax.fori_loop(0, 4, filter_inner, 0, unroll=2)

    along_grp(0)

    def convolve(i, carry):
        at = pl.ds(pl.multiple_of(i * 512, 512), 512)
        sig = inner_dot(high[at, :], low[at, :], 0)
        fil = spec[at, :]
        s_re, s_im = sig[:, :128], sig[:, 128:]
        f_re, f_im = fil[:, :128], fil[:, 128:]
        prod = jnp.concatenate([s_re * f_re - s_im * f_im, s_re * f_im + s_im * f_re], axis=1)
        p_h, p_l = halves(prod)
        back = inner_dot(p_h, p_l, 2)
        for j in range(8):
            re, im = back[64 * j : 64 * j + 64, :128], back[64 * j : 64 * j + 64, 128:]
            ct, st = twist[0], twist[1]
            t_h, t_l = halves(jnp.concatenate([re * ct - im * st, im * ct + re * st], axis=0))
            stage[pl.ds(pl.multiple_of(i * 512 + 64 * j, 64), 64), :] = dot(
                outer_inv[...], jnp.concatenate([t_h, t_h, t_l], axis=0))
        return carry

    settle(scales.at[pl.ds(0, N - 1)], r_aux)
    for part in range(PARTS):
        begin = WIDE * part
        settle(toks.at[pl.ds(0, N - 1), pl.ds(begin, WIDE)], r_tok.at[part])

        def load_signal(i, carry):
            tok = toks[i, begin : begin + WIDE].astype(F32)
            normed = (tok * scales[i] * chan[0, begin : begin + WIDE]).astype(BF16)
            stage[pl.ds(64 * begin + i, WIDE, stride=64), :] = normed.astype(F32)
            return carry

        lax.fori_loop(0, N, load_signal, 0, unroll=4)
        transform(outer_sig, WIDE // 8 * part, WIDE // 8 * (part + 1))
        lax.fori_loop(WIDE // 8 * part, WIDE // 8 * (part + 1), convolve, 0)

    along_grp(1)

    settle(targets.at[pl.ds(0, N - 1)], r_tgt)
    slot_ids = lax.broadcasted_iota(jnp.int32, (256, 128), 0).astype(F32)

    def pack(cls, part):
        picks = []
        for j in range(4):
            idx = cls * 16 + part * 4 + j
            tok = toks[idx].astype(F32)
            normed = (tok * scales[idx] * chan[0]).astype(BF16).astype(F32)
            conv = stage[pl.ds(idx, 32, stride=64), :]
            conv_out = (conv + chan[1] * normed).astype(BF16).astype(F32)
            diag[32 * j : 32 * j + 32, 128 * j : 128 * j + 128] = (tok + conv_out).astype(BF16)
            picks.append(jnp.where(slot_ids == targets[idx], 1.0, 0.0).astype(BF16))
        picked = lax.dot_general(
            jnp.concatenate(picks, axis=1), diag[...], (((1,), (1,)), ((), ())),
            preferred_element_type=F32)
        packed[cls, :, 16 * part : 16 * part + 16, :] = picked.astype(BF16).reshape(16, 16, 128)

    for half in range(2):

        def pack_class(i, carry):
            cls = lax.rem(group + i, 4)
            pack(cls, 2 * half)
            pack(cls, 2 * half + 1)
            part = pl.ds(32 * half, 32)

            def send(t, carry):
                to = lax.rem(expert + t, 16)
                dest = holder_of(cls, to)

                @pl.when(dest != me)
                def _():
                    pltpu.make_async_remote_copy(
                        packed.at[cls, to, part], rows.at[me, part], s_row.at[half],
                        r_row.at[half], device_id={"ctx": dest}, device_id_type=MESH).start()
                return carry

            lax.fori_loop(0, 16, send, 0)
            return carry

        lax.fori_loop(0, 4, pack_class, 0)
        if half == 0:
            to_partner(0)

    rows[pl.ds(me, 1)] = packed[group, pl.ds(expert, 1)]

    to_partner(1)

    lane = lax.broadcasted_iota(jnp.int32, (16, 128), 1)
    in_half, in_quarter = lane < 64, lane % 64 < 32
    for half in range(2):
        part = pl.ds(32 * half, 32)
        these = pl.ds(128 * half, 128)
        settle(rows.at[pl.ds(0, N - 1), part], r_row.at[half])

        def unpack(i, carry):
            at = pl.ds(pl.multiple_of(i * 128, 128), 128)
            for r in (2 * half, 2 * half + 1):
                v = [rows[4 * i + j, 16 * r : 16 * r + 16, :].astype(F32) for j in range(4)]
                a0 = jnp.where(in_half, v[0], pltpu.roll(v[2], 64, 1))
                a1 = jnp.where(in_half, v[1], pltpu.roll(v[3], 64, 1))
                a2 = jnp.where(in_half, pltpu.roll(v[0], 64, 1), v[2])
                a3 = jnp.where(in_half, pltpu.roll(v[1], 64, 1), v[3])
                u = [
                    jnp.where(in_quarter, a0, pltpu.roll(a1, 32, 1)),
                    jnp.where(in_quarter, pltpu.roll(a0, 96, 1), a1),
                    jnp.where(in_quarter, a2, pltpu.roll(a3, 32, 1)),
                    jnp.where(in_quarter, pltpu.roll(a2, 96, 1), a3),
                ]
                for p in range(4):
                    mid[64 * r + 16 * p : 64 * r + 16 * p + 16, at] = u[p]
            return carry

        lax.fori_loop(0, 16, unpack, 0, unroll=2)

        def norm_rows(i, carry):
            at = pl.ds(pl.multiple_of(i * 32, 32), 32)
            block = mid[at, :]
            scale = lax.rsqrt(
                jnp.sum(block * block, axis=1, keepdims=True) * (1.0 / 2048.0) + 1e-06)
            ffn_in[at, :] = (block * scale * gain_ffn[...]).astype(BF16)
            return carry

        lax.fori_loop(4 * half, 4 * half + 4, norm_rows, 0, unroll=2)
        logits = lax.dot_general(
            ffn_in[these, :], router[...], (((1,), (1,)), ((), ())), preferred_element_type=F32)
        chosen = lax.broadcasted_iota(jnp.int32, logits.shape, 1) == expert
        gate = jax.nn.sigmoid(jnp.sum(jnp.where(chosen, logits, 0.0), axis=1, keepdims=True))

        if half == 0:
            fetches[2].wait()
            fetches[3].wait()
            settle(up.at[1], r_w.at[10])
            settle(down.at[pl.ds(256, 256)], r_w.at[11])

        def go_up(i, carry):
            value = dot(ffn_in[these, :], up[i])
            value = value * (1.0 + lax.erf(value * math.sqrt(0.5))) * 0.5
            hidden[these, pl.ds(pl.multiple_of(i * 256, 256), 256)] = value.astype(BF16)
            return carry

        lax.fori_loop(0, 3, go_up, 0, unroll=3)
        if half == 0:
            settle(up.at[3], r_w.at[8])
        go_up(3, 0)
        if half == 0:
            settle(down.at[pl.ds(768, 256)], r_w.at[9])

        def go_down(i, carry):
            at = pl.ds(pl.multiple_of(i * 256, 256), 256)
            result = dot(hidden[these, :], down[:, at]).astype(BF16).astype(F32)
            value = (mid[these, at] + gate * result).astype(BF16)
            out_rows[8 * half : 8 * half + 8, :, at] = value.reshape(8, 16, 256)
            return carry

        lax.fori_loop(0, 8, go_down, 0, unroll=2)

        def send_out(i, carry):
            rank = 8 * half + lax.rem(my_rank + i, 8)

            @pl.when(rank != my_rank)
            def _():
                pltpu.make_async_remote_copy(
                    out_rows.at[rank], arrived.at[expert], s_out, r_out,
                    device_id={"ctx": source_of(me, rank)}, device_id_type=MESH).start()
            return carry

        lax.fori_loop(0, 8, send_out, 0)

    arrived[pl.ds(expert, 1)] = out_rows[pl.ds(my_rank, 1)]
    pick = jnp.where(slot_ids == target, 1.0, 0.0).T.astype(BF16)
    settle(arrived.at[pl.ds(0, 15)], r_out)

    for i in range(2):
        at = pl.ds(1024 * i, 1024)
        out[:, at] = dot(pick, arrived[:, :, at].reshape(256, 1024)).astype(BF16)

    settle(scales.at[pl.ds(0, N - 1)], s_aux)
    settle(targets.at[pl.ds(0, N - 1)], s_tgt)
    for part in range(PARTS):
        settle(toks.at[pl.ds(0, N - 1), pl.ds(WIDE * part, WIDE)], s_tok.at[part])
    for half in range(2):
        settle(rows.at[pl.ds(0, N - 1), pl.ds(32 * half, 32)], s_row.at[half])
    settle(arrived.at[pl.ds(0, 15)], s_out)
    for sem, ref in enumerate((
        held_up(0, 256), held_down(0, 32), held_up(256, 256), held_down(32, 32),
        up.at[2, pl.ds(0, 768)], down.at[pl.ds(512, 96)], up.at[2, pl.ds(0, 768)],
        down.at[pl.ds(512, 96)], up.at[3], down.at[pl.ds(768, 256)], up.at[1],
        down.at[pl.ds(256, 256)],
    )):
        settle(ref, s_w.at[sem])


def body(
    tokens, gain_in, long_filter, skip_gain, gain_ffn, router, w_up, w_down, expert_id, slot_index
):
    t = tables()
    consts = [jnp.asarray(t[k]) for k in ("twist", "outer_filt", "outer_sig", "outer_inv", "inner")]
    vmem = pl.BlockSpec(memory_space=pltpu.VMEM)
    anywhere = pl.BlockSpec(memory_space=pl.ANY)
    dma = pltpu.SemaphoreType.DMA
    return pl.pallas_call(
        kernel,
        out_shape=jax.ShapeDtypeStruct((128, 2048), BF16),
        in_specs=[vmem] * 5 + [anywhere] + [vmem] * 2 + [anywhere] * 2 + [vmem] * 4 + [anywhere],
        out_specs=vmem,
        scratch_shapes=[
            pltpu.VMEM((2, 32, 128), F32),
            pltpu.VMEM((128, 128), F32),
            pltpu.VMEM((N, 32, 128), BF16),
            pltpu.VMEM((2, 1, 128), F32),
            pltpu.VMEM((N, 32, 128), BF16),
            pltpu.VMEM((N, 1, 128), F32),
            pltpu.VMEM((N, 1, 128), F32),
            pltpu.VMEM((32, 8192), BF16),
            pltpu.VMEM((4, 256, 256), BF16),
            pltpu.VMEM((2048, 128), F32),
            pltpu.VMEM((2048, 256), F32),
            pltpu.VMEM((2048, 256), BF16),
            pltpu.VMEM((2048, 256), BF16),
            pltpu.VMEM((128, 512), BF16),
            pltpu.VMEM((4, 16, 64, 128), BF16),
            pltpu.VMEM((N, 64, 128), BF16),
            pltpu.VMEM((256, 2048), F32),
            pltpu.VMEM((256, 2048), BF16),
            pltpu.VMEM((256, 1024), BF16),
            pltpu.VMEM((16, 16, 2048), BF16),
            pltpu.VMEM((16, 16, 2048), BF16),
            pltpu.VMEM((4, 2048, 256), BF16),
            pltpu.VMEM((1024, 2048), BF16),
            dma((PARTS,)), dma((PARTS,)), dma, dma, dma, dma, dma((2,)), dma((2,)), dma, dma, dma((12,)),
            dma((12,)),
            dma((4,)),
        ],
        compiler_params=pltpu.CompilerParams(
            collective_id=0, has_side_effects=True, vmem_limit_bytes=60 * 1024 * 1024),
    )(
        tokens, expert_id.reshape(1, 128), slot_index.reshape(1, 128),
        gain_in.reshape(16, 128), skip_gain.reshape(1, 32), long_filter,
        gain_ffn.reshape(1, 2048), router.T, w_up, w_down, *consts
    )


def solution(mesh):
    return jax.shard_map(
        body,
        mesh=mesh,
        in_specs=(
            P(("grp", "ctx"), None),
            P(),
            P("ctx", None),
            P("ctx"),
            P(),
            P(),
            P(None, "ctx"),
            P("ctx", None),
            P(("grp", "ctx")),
            P(("grp", "ctx")),
        ),
        out_specs=P(("grp", "ctx"), None),
        check_vma=False,
    )
```

```python
import functools
import math

import jax
import jax.numpy as jnp
import numpy as np
from jax import lax
from jax.experimental import pallas as pl
from jax.experimental.pallas import tpu as pltpu
from jax.sharding import PartitionSpec as P

MESH = pl.DeviceIdType.MESH
F32, BF16 = jnp.float32, jnp.bfloat16
N = 64
GRP = 8
PARTS = 2
WIDE = 32 // PARTS
FAR_FIRST = (4, 3, 5, 2, 6, 1, 7, 0)


def class_of(dev):
    z, x, core = dev // 8, dev // 2 % 4, dev % 2
    return (x + x // 2) % 2 * 2 + core, (x // 2 + z) % 2 * 8 + z


def source_of(dev, rank):
    x, core = dev // 2 % 4, dev % 2
    parity = (x + x // 2) % 2
    side = (rank // 8 + rank) % 2
    return (rank % 8 * 4 + parity + side * (3 - 2 * parity)) * 2 + core


def holder_of(group, expert):
    parity, core, pair = group // 2, group % 2, expert % 2
    return (expert // 2 * 4 + 2 * pair + (parity + pair) % 2) * 2 + core


def split(table):
    high = table.astype(np.float32).astype(BF16)
    low = (table - high.astype(np.float64)).astype(np.float32).astype(BF16)
    return high, low


@functools.lru_cache(None)
def tables():
    place = np.arange(N)
    parity, core, rank = place // 32, place // 16 % 2, place % 16
    side = (rank // 8 + rank) % 2
    order = (rank % 8 * 4 + parity + side * (3 - 2 * parity)) * 2 + core
    quarter = 4 * np.arange(64) + 1
    lane = np.arange(128)

    def angle(first, second, period):
        return 2.0 * math.pi * (np.outer(first, second) % period) / period

    twist = angle(quarter, lane, 32768)
    inner = angle(lane, lane, 128)
    ci, si = np.cos(inner), np.sin(inner)
    out = {"twist": np.stack([np.cos(twist), np.sin(twist)]).astype(np.float32)}
    for name, blocks in (("filt", np.arange(64)), ("sig", order)):
        theta = angle(quarter, blocks, 256)
        high, low = split(np.concatenate([np.cos(theta), -np.sin(theta)], axis=0))
        out["outer_" + name] = np.concatenate([high, low], axis=1)
    theta = angle(order, quarter, 256)
    high, low = split(np.concatenate([np.cos(theta), -np.sin(theta)], axis=1) / 8192.0)
    out["outer_inv"] = np.concatenate([high, low, high], axis=1)
    out["inner"] = np.stack(
        split(np.block([[ci, -si], [si, ci]])) + split(np.block([[ci, si], [-si, ci]])))
    return out


def dot(left, right):
    return jnp.dot(left, right, preferred_element_type=F32)


def halves(value):
    high = value.astype(BF16)
    return high, (value - high.astype(F32)).astype(BF16)


def settle(ref, sem):
    pltpu.make_async_copy(ref, ref, sem).wait()


def kernel(
    tokens, expert_id, slot_index, gain_in, skip_gain, filt_hbm, gain_ffn, router, w_up, w_down,
    twist, outer_filt, outer_sig, outer_inv, inner_hbm,
    out,
    chan, turned_gain, toks_t, aux, toks, scales, targets, filt, inner, stage, spec, high, low, diag, packed, rows, mid,
    ffn_in, hidden, out_rows, arrived, up, down,
    s_tok, r_tok, s_aux, r_aux, s_tgt, r_tgt, s_row, r_row, s_out, r_out, s_w, r_w, local,
):
    me = lax.axis_index("ctx")
    grp = lax.axis_index("grp")
    group, my_rank = class_of(me)
    place = group * 16 + my_rank
    expert = me // 4
    partner = me // 2 * 2 + 1 - me % 2
    across = me // 4 * 4 + (me + 2) % 4
    ahead, behind = lax.rem(grp + 1, GRP), lax.rem(grp + GRP - 1, GRP)
    ahead2, behind2 = lax.rem(grp + 2, GRP), lax.rem(grp + GRP - 2, GRP)

    barrier = pltpu.get_barrier_semaphore()

    def greet(i, carry):
        pl.semaphore_signal(
            barrier, inc=1, device_id={"ctx": lax.rem(me + i, N)}, device_id_type=MESH)
        return carry

    lax.fori_loop(1, N, greet, 0, unroll=7)
    for neighbour in (ahead, behind, ahead2, behind2):
        pl.semaphore_signal(barrier, inc=1, device_id={"grp": neighbour}, device_id_type=MESH)

    fetches = [
        pltpu.make_async_copy(filt_hbm, filt, local.at[0]),
        pltpu.make_async_copy(inner_hbm, inner, local.at[1]),
        pltpu.make_async_copy(w_up, up.at[0], local.at[2]),
        pltpu.make_async_copy(w_down, down.at[pl.ds(0, 256)], local.at[3]),
    ]
    for fetch in fetches:
        fetch.start()

    total = jnp.zeros((1, 128), F32)
    for j in range(16):
        block = tokens[:, 128 * j : 128 * j + 128].astype(F32).T
        total = total + jnp.sum(block * block, axis=0, keepdims=True)
        toks_t[4 * j : 4 * j + 4] = block.astype(BF16).reshape(4, 32, 128)
    target = (expert_id[...] * 16 + slot_index[...]).astype(F32)
    aux[0] = lax.rsqrt(total * (1.0 / 2048.0) + 1e-06)
    aux[1] = target
    row = gain_in[pl.ds(me // 4, 1), :]
    turned_gain[...] = jnp.broadcast_to(row, (128, 128)).T
    chan[0] = turned_gain[pl.ds(pl.multiple_of(me % 4 * 32, 32), 32), :]
    chan[1] = jnp.broadcast_to(skip_gain[...], (128, 32)).T
    pl.semaphore_wait(barrier, N + 3)

    def push(source, dest, sem, device):
        pltpu.make_async_remote_copy(
            source, dest, s_w.at[sem], r_w.at[sem], device_id=device, device_id_type=MESH
        ).start()

    quarter = lax.rem(grp, 4)
    up_at = pl.multiple_of(quarter * 512, 512)
    down_at = pl.multiple_of(quarter * 64, 64)

    def held_up(first, count):
        return up.at[2, pl.ds(up_at + first, count)]

    def held_down(first, count):
        return down.at[pl.ds(512 + down_at + first, count)]

    def over_x(piece):
        push(
            w_up.at[pl.ds(up_at + 256 * piece, 256)], held_up(256 * piece, 256), 2 * piece,
            {"ctx": across})
        push(
            w_down.at[pl.ds(down_at + 32 * piece, 32)], held_down(32 * piece, 32),
            2 * piece + 1, {"ctx": across})

    def along_grp(piece):
        settle(held_up(256 * piece, 256), r_w.at[2 * piece])
        settle(held_down(32 * piece, 32), r_w.at[2 * piece + 1])
        for first, device in ((0, ahead2), (1, behind2)):
            some_up = held_up(256 * piece + 128 * first, 128)
            some_down = held_down(32 * piece + 16 * first, 16)
            push(some_up, some_up, 4 + 2 * piece, {"grp": device})
            push(some_down, some_down, 5 + 2 * piece, {"grp": device})
        for device in (ahead, behind):
            some_up, some_down = held_up(256 * piece, 256), held_down(32 * piece, 32)
            push(some_up, some_up, 4 + 2 * piece, {"grp": device})
            push(some_down, some_down, 5 + 2 * piece, {"grp": device})

    def to_partner(piece):
        settle(up.at[2, pl.ds(0, 768)], r_w.at[4 + 2 * piece])
        settle(down.at[pl.ds(512, 96)], r_w.at[5 + 2 * piece])
        for q in range(4):
            rows_at = pl.ds(512 * q + 256 * piece, 256)
            push(up.at[2, rows_at], up.at[3, rows_at], 8, {"ctx": partner})
            first = 64 * q + 32 * piece
            push(
                down.at[pl.ds(512 + first, 32)], down.at[pl.ds(768 + first, 32)], 9,
                {"ctx": partner})

    over_x(0)

    def send_aux(which, dest, s_sem, r_sem):
        def send(i, carry):
            pltpu.make_async_remote_copy(
                aux.at[which], dest.at[place], s_sem, r_sem,
                device_id={"ctx": lax.rem(me + i, N)}, device_id_type=MESH).start()
            return carry

        lax.fori_loop(1, N, send, 0, unroll=7)

    def send_toks(part, carry):
        channels = pl.ds(pl.multiple_of(WIDE * part, WIDE), WIDE)

        def send(i, carry):
            peer = lax.rem(me + i, N)
            pltpu.make_async_remote_copy(
                toks_t.at[peer, channels], toks.at[place, channels], s_tok.at[part],
                r_tok.at[part], device_id={"ctx": peer}, device_id_type=MESH).start()
            return carry

        return lax.fori_loop(1, N, send, carry, unroll=7)

    send_aux(0, scales, s_aux, r_aux)
    lax.fori_loop(0, PARTS, send_toks, 0)
    over_x(1)
    send_aux(1, targets, s_tgt, r_tgt)
    push(w_up, up.at[1], 10, {"ctx": partner})
    push(w_down, down.at[pl.ds(256, 256)], 11, {"ctx": partner})
    toks[pl.ds(place, 1)] = toks_t[pl.ds(me, 1)]
    scales[place] = aux[0]
    targets[place] = aux[1]

    diag[...] = jnp.zeros_like(diag)

    def transform(outer, begin, end):
        def channels(i, carry):
            for j in range(8):
                at = pl.multiple_of((8 * i + j) * 64, 64)
                block = stage[pl.ds(at, 64), :].astype(BF16)
                first = dot(outer[...], jnp.concatenate([block, block], axis=0))
                re, im = first[:64], first[64:]
                ct, st = twist[0], twist[1]
                re_h, re_l = halves(re * ct + im * st)
                im_h, im_l = halves(im * ct - re * st)
                high[pl.ds(at, 64), 0:128] = re_h
                high[pl.ds(at, 64), 128:256] = im_h
                low[pl.ds(at, 64), 0:128] = re_l
                low[pl.ds(at, 64), 128:256] = im_l
            return carry

        lax.fori_loop(begin, end, channels, 0)

    def inner_dot(hi, lo, which):
        return dot(hi, inner[which]) + dot(hi, inner[which + 1]) + dot(lo, inner[which])

    def load_filter(i, carry):
        stage[pl.ds(i, 32, stride=64), :] = filt[
            :, pl.ds(pl.multiple_of(i * 128, 128), 128)].astype(F32)
        return carry

    fetches[0].wait()
    fetches[1].wait()
    lax.fori_loop(0, N, load_filter, 0, unroll=4)
    transform(outer_filt, 0, 4)

    def filter_inner(i, carry):
        at = pl.ds(pl.multiple_of(i * 512, 512), 512)
        spec[at, :] = inner_dot(high[at, :], low[at, :], 0)
        return carry

    lax.fori_loop(0, 4, filter_inner, 0, unroll=2)

    along_grp(0)

    def convolve(i, carry):
        at = pl.ds(pl.multiple_of(i * 512, 512), 512)
        sig = inner_dot(high[at, :], low[at, :], 0)
        fil = spec[at, :]
        s_re, s_im = sig[:, :128], sig[:, 128:]
        f_re, f_im = fil[:, :128], fil[:, 128:]
        prod = jnp.concatenate([s_re * f_re - s_im * f_im, s_re * f_im + s_im * f_re], axis=1)
        p_h, p_l = halves(prod)
        back = inner_dot(p_h, p_l, 2)
        for j in range(8):
            re, im = back[64 * j : 64 * j + 64, :128], back[64 * j : 64 * j + 64, 128:]
            ct, st = twist[0], twist[1]
            t_h, t_l = halves(jnp.concatenate([re * ct - im * st, im * ct + re * st], axis=0))
            stage[pl.ds(pl.multiple_of(i * 512 + 64 * j, 64), 64), :] = dot(
                outer_inv[...], jnp.concatenate([t_h, t_h, t_l], axis=0))
        return carry

    settle(scales.at[pl.ds(0, N - 1)], r_aux)
    for part in range(PARTS):
        begin = WIDE * part
        settle(toks.at[pl.ds(0, N - 1), pl.ds(begin, WIDE)], r_tok.at[part])

        def load_signal(i, carry):
            tok = toks[i, begin : begin + WIDE].astype(F32)
            normed = (tok * scales[i] * chan[0, begin : begin + WIDE]).astype(BF16)
            stage[pl.ds(64 * begin + i, WIDE, stride=64), :] = normed.astype(F32)
            return carry

        lax.fori_loop(0, N, load_signal, 0, unroll=4)
        transform(outer_sig, WIDE // 8 * part, WIDE // 8 * (part + 1))
        lax.fori_loop(WIDE // 8 * part, WIDE // 8 * (part + 1), convolve, 0)

    along_grp(1)

    settle(targets.at[pl.ds(0, N - 1)], r_tgt)
    slot_ids = lax.broadcasted_iota(jnp.int32, (256, 128), 0).astype(F32)

    def pack(cls, part):
        picks = []
        for j in range(4):
            idx = cls * 16 + part * 4 + j
            tok = toks[idx].astype(F32)
            normed = (tok * scales[idx] * chan[0]).astype(BF16).astype(F32)
            conv = stage[pl.ds(idx, 32, stride=64), :]
            conv_out = (conv + chan[1] * normed).astype(BF16).astype(F32)
            diag[32 * j : 32 * j + 32, 128 * j : 128 * j + 128] = (tok + conv_out).astype(BF16)
            picks.append(jnp.where(slot_ids == targets[idx], 1.0, 0.0).astype(BF16))
        picked = lax.dot_general(
            jnp.concatenate(picks, axis=1), diag[...], (((1,), (1,)), ((), ())),
            preferred_element_type=F32)
        packed[cls, :, 16 * part : 16 * part + 16, :] = picked.astype(BF16).reshape(16, 16, 128)

    for half in range(2):

        def pack_class(i, carry):
            cls = lax.rem(group + i, 4)
            pack(cls, 2 * half)
            pack(cls, 2 * half + 1)
            part = pl.ds(32 * half, 32)

            def send(to):
                dest = holder_of(cls, to)

                @pl.when(dest != me)
                def _():
                    pltpu.make_async_remote_copy(
                        packed.at[cls, to, part], rows.at[me, part], s_row.at[half],
                        r_row.at[half], device_id={"ctx": dest}, device_id_type=MESH).start()

            for offset in FAR_FIRST:
                for pair in range(2):
                    send(lax.rem(me // 8 + offset, 8) * 2 + pair)
            return carry

        lax.fori_loop(0, 4, pack_class, 0)
        if half == 0:
            to_partner(0)

    rows[pl.ds(me, 1)] = packed[group, pl.ds(expert, 1)]

    to_partner(1)

    lane = lax.broadcasted_iota(jnp.int32, (16, 128), 1)
    in_half, in_quarter = lane < 64, lane % 64 < 32
    for half in range(2):
        part = pl.ds(32 * half, 32)
        these = pl.ds(128 * half, 128)
        settle(rows.at[pl.ds(0, N - 1), part], r_row.at[half])

        def unpack(i, carry):
            at = pl.ds(pl.multiple_of(i * 128, 128), 128)
            for r in (2 * half, 2 * half + 1):
                v = [rows[4 * i + j, 16 * r : 16 * r + 16, :].astype(F32) for j in range(4)]
                a0 = jnp.where(in_half, v[0], pltpu.roll(v[2], 64, 1))
                a1 = jnp.where(in_half, v[1], pltpu.roll(v[3], 64, 1))
                a2 = jnp.where(in_half, pltpu.roll(v[0], 64, 1), v[2])
                a3 = jnp.where(in_half, pltpu.roll(v[1], 64, 1), v[3])
                u = [
                    jnp.where(in_quarter, a0, pltpu.roll(a1, 32, 1)),
                    jnp.where(in_quarter, pltpu.roll(a0, 96, 1), a1),
                    jnp.where(in_quarter, a2, pltpu.roll(a3, 32, 1)),
                    jnp.where(in_quarter, pltpu.roll(a2, 96, 1), a3),
                ]
                for p in range(4):
                    mid[64 * r + 16 * p : 64 * r + 16 * p + 16, at] = u[p]
            return carry

        lax.fori_loop(0, 16, unpack, 0, unroll=2)

        def norm_rows(i, carry):
            at = pl.ds(pl.multiple_of(i * 32, 32), 32)
            block = mid[at, :]
            scale = lax.rsqrt(
                jnp.sum(block * block, axis=1, keepdims=True) * (1.0 / 2048.0) + 1e-06)
            ffn_in[at, :] = (block * scale * gain_ffn[...]).astype(BF16)
            return carry

        lax.fori_loop(4 * half, 4 * half + 4, norm_rows, 0, unroll=2)
        logits = lax.dot_general(
            ffn_in[these, :], router[...], (((1,), (1,)), ((), ())), preferred_element_type=F32)
        chosen = lax.broadcasted_iota(jnp.int32, logits.shape, 1) == expert
        gate = jax.nn.sigmoid(jnp.sum(jnp.where(chosen, logits, 0.0), axis=1, keepdims=True))

        if half == 0:
            fetches[2].wait()
            fetches[3].wait()
            settle(up.at[1], r_w.at[10])
            settle(down.at[pl.ds(256, 256)], r_w.at[11])
            settle(up.at[3], r_w.at[8])
            settle(down.at[pl.ds(768, 256)], r_w.at[9])

        def go_up(i, carry):
            value = dot(ffn_in[these, :], up[i])
            value = value * (1.0 + lax.erf(value * math.sqrt(0.5))) * 0.5
            hidden[these, pl.ds(pl.multiple_of(i * 256, 256), 256)] = value.astype(BF16)
            return carry

        lax.fori_loop(0, 4, go_up, 0, unroll=2)

        def go_down(i, carry):
            at = pl.ds(pl.multiple_of(i * 256, 256), 256)
            result = dot(hidden[these, :], down[:, at]).astype(BF16).astype(F32)
            value = (mid[these, at] + gate * result).astype(BF16)
            out_rows[8 * half : 8 * half + 8, :, at] = value.reshape(8, 16, 256)
            return carry

        lax.fori_loop(0, 8, go_down, 0, unroll=2)

        def send_out(offset):
            rank = 8 * half + lax.rem(my_rank + offset, 8)

            @pl.when(rank != my_rank)
            def _():
                pltpu.make_async_remote_copy(
                    out_rows.at[rank], arrived.at[expert], s_out, r_out,
                    device_id={"ctx": source_of(me, rank)}, device_id_type=MESH).start()

        for offset in FAR_FIRST:
            send_out(offset)

    arrived[pl.ds(expert, 1)] = out_rows[pl.ds(my_rank, 1)]
    pick = jnp.where(slot_ids == target, 1.0, 0.0).T.astype(BF16)
    settle(arrived.at[pl.ds(0, 15)], r_out)

    for i in range(2):
        at = pl.ds(1024 * i, 1024)
        out[:, at] = dot(pick, arrived[:, :, at].reshape(256, 1024)).astype(BF16)

    settle(scales.at[pl.ds(0, N - 1)], s_aux)
    settle(targets.at[pl.ds(0, N - 1)], s_tgt)
    for part in range(PARTS):
        settle(toks.at[pl.ds(0, N - 1), pl.ds(WIDE * part, WIDE)], s_tok.at[part])
    for half in range(2):
        settle(rows.at[pl.ds(0, N - 1), pl.ds(32 * half, 32)], s_row.at[half])
    settle(arrived.at[pl.ds(0, 15)], s_out)
    for sem, ref in enumerate((
        held_up(0, 256), held_down(0, 32), held_up(256, 256), held_down(32, 32),
        up.at[2, pl.ds(0, 768)], down.at[pl.ds(512, 96)], up.at[2, pl.ds(0, 768)],
        down.at[pl.ds(512, 96)], up.at[3], down.at[pl.ds(768, 256)], up.at[1],
        down.at[pl.ds(256, 256)],
    )):
        settle(ref, s_w.at[sem])


def body(
    tokens, gain_in, long_filter, skip_gain, gain_ffn, router, w_up, w_down, expert_id, slot_index
):
    t = tables()
    consts = [jnp.asarray(t[k]) for k in ("twist", "outer_filt", "outer_sig", "outer_inv", "inner")]
    vmem = pl.BlockSpec(memory_space=pltpu.VMEM)
    anywhere = pl.BlockSpec(memory_space=pl.ANY)
    dma = pltpu.SemaphoreType.DMA
    return pl.pallas_call(
        kernel,
        out_shape=jax.ShapeDtypeStruct((128, 2048), BF16),
        in_specs=[vmem] * 5 + [anywhere] + [vmem] * 2 + [anywhere] * 2 + [vmem] * 4 + [anywhere],
        out_specs=vmem,
        scratch_shapes=[
            pltpu.VMEM((2, 32, 128), F32),
            pltpu.VMEM((128, 128), F32),
            pltpu.VMEM((N, 32, 128), BF16),
            pltpu.VMEM((2, 1, 128), F32),
            pltpu.VMEM((N, 32, 128), BF16),
            pltpu.VMEM((N, 1, 128), F32),
            pltpu.VMEM((N, 1, 128), F32),
            pltpu.VMEM((32, 8192), BF16),
            pltpu.VMEM((4, 256, 256), BF16),
            pltpu.VMEM((2048, 128), F32),
            pltpu.VMEM((2048, 256), F32),
            pltpu.VMEM((2048, 256), BF16),
            pltpu.VMEM((2048, 256), BF16),
            pltpu.VMEM((128, 512), BF16),
            pltpu.VMEM((4, 16, 64, 128), BF16),
            pltpu.VMEM((N, 64, 128), BF16),
            pltpu.VMEM((256, 2048), F32),
            pltpu.VMEM((256, 2048), BF16),
            pltpu.VMEM((256, 1024), BF16),
            pltpu.VMEM((16, 16, 2048), BF16),
            pltpu.VMEM((16, 16, 2048), BF16),
            pltpu.VMEM((4, 2048, 256), BF16),
            pltpu.VMEM((1024, 2048), BF16),
            dma((PARTS,)), dma((PARTS,)), dma, dma, dma, dma, dma((2,)), dma((2,)), dma, dma, dma((12,)),
            dma((12,)),
            dma((4,)),
        ],
        compiler_params=pltpu.CompilerParams(
            collective_id=0, has_side_effects=True, vmem_limit_bytes=60 * 1024 * 1024),
    )(
        tokens, expert_id.reshape(1, 128), slot_index.reshape(1, 128),
        gain_in.reshape(16, 128), skip_gain.reshape(1, 32), long_filter,
        gain_ffn.reshape(1, 2048), router.T, w_up, w_down, *consts
    )


def solution(mesh):
    return jax.shard_map(
        body,
        mesh=mesh,
        in_specs=(
            P(("grp", "ctx"), None),
            P(),
            P("ctx", None),
            P("ctx"),
            P(),
            P(),
            P(None, "ctx"),
            P("ctx", None),
            P(("grp", "ctx")),
            P(("grp", "ctx")),
        ),
        out_specs=P(("grp", "ctx"), None),
        check_vma=False,
    )
```
